1024 devices in a mesh: dp: 16 (over x, y), fsdp: 64 (over z, core).
Axes of the slice: x: 4, y: 4, z: 32, core: 2. Of those that a mesh axis runs over, the one named last changes fastest.
Arguments:
- grads: bfloat16 [16, 128, 512, 512], P('dp', None, 'fsdp'), may hold values from -4 to 4
- left_stats: float32 [64, 4, 512, 512], P('fsdp', None, 'dp'), may hold values from -0.5 to 9, as said below
- right_stats: float32 [64, 4, 512, 512], P('fsdp', None, 'dp'), may hold values from -0.5 to 9, as said below
- left_root: bfloat16 [64, 4, 512, 512], P('fsdp', None, 'dp'), may hold values from -0.5 to 14, as said below
- right_root: bfloat16 [64, 4, 512, 512], P('fsdp'), may hold values from -0.5 to 14, as said below
- second_moment: float32 [64, 4, 512, 512], P('fsdp', None, 'dp'), may hold values from 0.2 to 2
- slot_block: int32 [64, 4], replicated, may hold values from 0 to 127, as said below
- counts: int32 [64], replicated, may hold values from 0 to 4, as said below
Outputs:
- left_new: float32 [64, 4, 512, 512], P('fsdp', None, 'dp')
- right_new: float32 [64, 4, 512, 512], P('fsdp', None, 'dp')
- second_new: float32 [64, 4, 512, 512], P('fsdp', None, 'dp')
- update: float32 [64, 4, 512, 512], P('fsdp', None, 'dp')
The draws below stay inside these ranges and needn't reach their ends.
Inputs may be any that keep to these rules, and one draw needn't show every extreme that they name: Every owner holds counts[o] blocks; the counts sum to 128, and some owner holds exactly 4. `slot_block`: the first counts[o] slots of owner o name distinct blocks, every block is named by exactly one such slot, and later slots name arbitrary blocks. `left_stats`: Symmetric. `right_stats`: Symmetric. `left_root`: Symmetric. `right_root`: Symmetric.
All inputs are finite; a program needn't handle non-finite values.
Results may differ from the reference program's by a relative error of at most 0.015.
Values may be sent and summed in bfloat16 or wider, within the bound.
A program may use at most 32 MiB of HBM per device.

```python
import math
import jax
import jax.numpy as jnp
from jax import lax

BS = 512
BLK_OWN = 2
CAP = 4
NB = 128
N_DP = 16
N_FSDP = 64


def symmetric_blocks(key, low_end, high_end):
    noise_key, diag_key = jax.random.split(key, 2)
    block_shape = (N_FSDP, CAP, BS, BS)
    symmetric = jax.random.normal(noise_key, block_shape, jnp.float32)
    diagonal = jnp.exp(jax.random.uniform(diag_key, block_shape[:3], jnp.float32, jnp.log(low_end), jnp.log(high_end)))
    symmetric = (symmetric + jnp.swapaxes(symmetric, 2, 3)) * (0.45 / (2.0 * BS) ** 0.5)
    row_place = jnp.arange(BS, dtype=jnp.float32) / BS
    diagonal = diagonal * 3.0 ** row_place
    return symmetric + diagonal[..., None] * jnp.eye(BS, dtype=jnp.float32)


def ownership(key):
    base_key = jax.random.fold_in(key, 77)
    owner_key, shift_key, block_key = jax.random.split(base_key, 3)
    owners = jax.random.permutation(owner_key, N_FSDP)
    half_owners = N_FSDP // 2
    moved_blocks = jax.random.randint(shift_key, (half_owners,), 0, BLK_OWN + 1)
    moved_blocks = moved_blocks.at[0].set(BLK_OWN)
    held = jnp.full((N_FSDP,), BLK_OWN, jnp.int32)
    held = held.at[owners[:half_owners]].add(moved_blocks).at[owners[half_owners:]].add(-moved_blocks)
    blocks = jax.random.permutation(block_key, NB)
    offsets = jnp.cumsum(held) - held
    slot_place = (offsets[:, None] + jnp.arange(CAP)[None, :]) % NB
    return (held.astype(jnp.int32), blocks[slot_place].astype(jnp.int32))


def draw_left_stats(key, part):
    return symmetric_blocks(jax.random.fold_in(key, 1), 0.5, 2.0)


def draw_right_stats(key, part):
    return symmetric_blocks(jax.random.fold_in(key, 2), 0.5, 2.0)


def draw_left_root(key, part):
    return symmetric_blocks(jax.random.fold_in(key, 3), 1.0, 3.3).astype(jnp.bfloat16)


def draw_right_root(key, part):
    return symmetric_blocks(jax.random.fold_in(key, 4), 1.0, 3.3).astype(jnp.bfloat16)


def draw_slot_block(key, part):
    return ownership(key)[1]


def draw_counts(key, part):
    return ownership(key)[0]


def block_scale(key, shape, shards, least, top_value):
    gain, own = 1.0, jax.random.fold_in(key, 6)
    for axis_at, blocks in shards:
        heights = jnp.exp(jax.random.uniform(jax.random.fold_in(own, axis_at), (blocks,), jnp.float32, least / len(shards), top_value / len(shards)))
        gain = gain * jnp.repeat(heights, shape[axis_at] // blocks).reshape([-1 if axis == axis_at else 1 for axis in range(len(shape))])
    return gain


def centred(rng, extent, scale, reach, pieces=(), kind=jnp.bfloat16):
    result = scale * jax.random.normal(rng, extent, jnp.float32)
    if pieces:
        result = result * block_scale(rng, extent, pieces, -0.22, 0.18)
    return jnp.clip(result, -reach, reach).astype(kind)


def setup_inputs(seed: int = 0) -> dict:
    arg_keys = jax.random.split(jax.random.key(seed), 9)
    grads = centred(arg_keys[0], (N_DP, NB, BS, BS), 0.25, 4.0, ((0, 16), (2, 64)))
    left_stats = draw_left_stats(jax.random.fold_in(arg_keys[8], 71), 0)
    right_stats = draw_right_stats(jax.random.fold_in(arg_keys[8], 71), 0)
    left_root = draw_left_root(jax.random.fold_in(arg_keys[8], 71), 0)
    right_root = draw_right_root(jax.random.fold_in(arg_keys[8], 71), 0)
    second_moment = jnp.clip(jnp.exp(math.log(2.0) - 2.3025851 * jax.random.uniform(arg_keys[5], (N_FSDP, CAP, BS, BS), jnp.float32) ** block_scale(arg_keys[5], (N_FSDP, CAP, BS, BS), ((0, 64), (2, 16)), -0.2, 0.2)), 0.2, 2.0)
    slot_block = draw_slot_block(jax.random.fold_in(arg_keys[8], 71), 0)
    counts = draw_counts(jax.random.fold_in(arg_keys[8], 71), 0)
    return {"grads": grads, "left_stats": left_stats, "right_stats": right_stats, "left_root": left_root, "right_root": right_root, "second_moment": second_moment, "slot_block": slot_block, "counts": counts}


SHAMPOO_BETA = 0.998
ADAM_BETA = 0.95
EPSILON = 1e-08

def reference(grads, left_stats, right_stats, left_root, right_root, second_moment, slot_block, counts):

    def accumulate(step_index, grad_total):
        return grad_total + grads[step_index].astype(jnp.float32)
    grad_total = lax.fori_loop(0, N_DP, accumulate, jnp.zeros(grads.shape[1:], jnp.float32))
    grad_blocks = lax.optimization_barrier(grad_total.astype(jnp.bfloat16))
    live_slots = jnp.arange(CAP, dtype=jnp.int32)[None, :] < counts[:, None]
    keep_mask = live_slots[:, :, None, None]
    picked = jnp.where(keep_mask, grad_blocks[slot_block], jnp.zeros((), jnp.bfloat16))
    widened = picked.astype(jnp.float32)
    left_term = jnp.einsum('oaik,oajk->oaij', widened, widened)
    right_term = jnp.einsum('oaki,oakj->oaij', widened, widened)
    left_new = jnp.where(keep_mask, SHAMPOO_BETA * left_stats + (1.0 - SHAMPOO_BETA) * left_term, left_stats)
    right_new = jnp.where(keep_mask, SHAMPOO_BETA * right_stats + (1.0 - SHAMPOO_BETA) * right_term, right_stats)
    left_half = jnp.einsum('oaik,oakj->oaij', left_root.astype(jnp.float32), widened)
    left_half = lax.optimization_barrier(left_half.astype(jnp.bfloat16))
    precond = jnp.einsum('oaik,oakj->oaij', left_half.astype(jnp.float32), right_root.astype(jnp.float32))
    second_new = jnp.where(keep_mask, ADAM_BETA * second_moment + (1.0 - ADAM_BETA) * widened * widened, second_moment)
    adam = widened / (jnp.sqrt(second_new) + EPSILON)
    precond_sum = lax.optimization_barrier(jnp.sum(precond * precond, axis=(2, 3)))
    adam_sum = lax.optimization_barrier(jnp.sum(adam * adam, axis=(2, 3)))
    graft_scale = jnp.where(live_slots, jnp.sqrt(adam_sum / jnp.where(live_slots, precond_sum, 1.0)), 0.0)
    update = precond * graft_scale[:, :, None, None]
    return (left_new, right_new, second_new, update)
```

```python
import jax
import jax.numpy as jnp
from jax import lax
from jax.experimental import pallas as pl
from jax.experimental.pallas import tpu as pltpu
from jax.sharding import PartitionSpec as P

SHAMPOO_BETA = 0.998
ADAM_BETA = 0.95
EPSILON = 1e-08

SIDE = 4
LANES = 128
PART = LANES // SIDE
F32 = jnp.float32
BF16 = jnp.bfloat16


def kernel(
    n_fsdp,
    slot_ref,
    count_ref,
    grads,
    left_old,
    right_old,
    left_root,
    right_root,
    moment_old,
    left_out,
    right_out,
    moment_out,
    update_out,
    own_tile,
    first_in,
    stacked,
    perm,
    rep,
    second_send,
    second_in,
    table,
    message,
    gathered,
    lo_v,
    ro_v,
    lr_v,
    rr_v,
    mo_v,
    left_v,
    right_v,
    moment_v,
    update_v,
    lhs_v,
    half_v,
    term_v,
    own_v,
    norm_out,
    norm_in,
    load_sem,
    out_sem,
    first_send_sem,
    first_recv_sem,
    second_send_sem,
    second_recv_sem,
    swap_send_sem,
    swap_recv_sem,
    a_send_sem,
    a_recv_sem,
    b_send_sem,
    b_recv_sem,
    norm_send_sem,
    norm_recv_sem,
    from_left,
    from_right,
):
    dp = lax.axis_index("dp")
    owner = lax.axis_index("fsdp")
    gx, gy = dp // SIDE, dp % SIDE
    z, core = owner // 2, owner % 2
    n_z = n_fsdp // 2
    other = 1 - core
    i1 = gx * other + gy * core
    i2 = gy * other + gx * core

    def first_peer(k):
        return (((gx + k * other) % SIDE) * SIDE + (gy + k * core) % SIDE, owner)

    def second_peer(k):
        return (((gx + k * core) % SIDE) * SIDE + (gy + k * other) % SIDE, owner)

    def x_peer(k):
        return (((gx + k) % SIDE) * SIDE + gy, owner)

    def y_peer(k):
        return (gx * SIDE + (gy + k) % SIDE, owner)

    def z_peer(k):
        return (dp, ((z + k + n_z) % n_z) * 2 + core)

    def remote(src, dst, send, recv, peer):
        return pltpu.make_async_remote_copy(
            src_ref=src,
            dst_ref=dst,
            send_sem=send,
            recv_sem=recv,
            device_id=peer,
            device_id_type=pl.DeviceIdType.MESH,
        )

    own_load = pltpu.make_async_copy(
        grads.at[0, :, :, pl.ds(pl.multiple_of(i1 * LANES, LANES), LANES)], own_tile, load_sem.at[0]
    )
    own_load.start()

    barrier = pltpu.get_barrier_semaphore()
    greeted = [x_peer(k) for k in range(1, SIDE)] + [y_peer(k) for k in range(1, SIDE)]
    greeted += [z_peer(1), z_peer(-1), (dp, z * 2 + other)]
    for peer in greeted:
        pl.semaphore_signal(barrier, inc=1, device_id=peer, device_id_type=pl.DeviceIdType.MESH)
    loads = [
        pltpu.make_async_copy(src.at[0], dst, load_sem.at[1 + n])
        for n, (src, dst) in enumerate(
            ((left_old, lo_v), (right_old, ro_v), (left_root, lr_v), (right_root, rr_v), (moment_old, mo_v))
        )
    ]
    for load in loads:
        load.start()
    pl.semaphore_wait(barrier, len(greeted))

    first = []
    for k in (2, 1, 3):
        tile = pl.ds(pl.multiple_of(((i1 + k) % SIDE) * LANES, LANES), LANES)
        copy = remote(
            grads.at[0, :, :, tile],
            first_in.at[k - 1],
            first_send_sem.at[k - 1],
            first_recv_sem.at[k - 1],
            first_peer(k),
        )
        copy.start()
        first.append(copy)

    row = lax.broadcasted_iota(jnp.int32, (SIDE * LANES, SIDE * LANES), 0)
    col = lax.broadcasted_iota(jnp.int32, (SIDE * LANES, SIDE * LANES), 1)
    want = ((col % LANES) // PART) * LANES + (col // LANES) * PART + col % PART
    perm[...] = jnp.where(row == want, 1.0, 0.0).astype(BF16)
    row = lax.broadcasted_iota(jnp.int32, (LANES, SIDE * LANES), 0)
    col = lax.broadcasted_iota(jnp.int32, (LANES, SIDE * LANES), 1)
    rep[...] = jnp.where(row == (col // LANES) * PART + col % PART, 1.0, 0.0).astype(BF16)
    table[pl.ds(SIDE * 32, 1)] = jnp.zeros((1, 8, LANES), F32)

    def meet(step, carry):
        pl.semaphore_signal(from_left, inc=1, device_id=z_peer(1), device_id_type=pl.DeviceIdType.MESH)
        pl.semaphore_signal(from_right, inc=1, device_id=z_peer(-1), device_id_type=pl.DeviceIdType.MESH)
        pl.semaphore_wait(from_left, 1)
        pl.semaphore_wait(from_right, 1)
        return carry

    lax.fori_loop(0, n_z // 2, meet, 0)

    own_load.wait()
    for copy in first:
        copy.wait_recv()
    quads = own_tile.shape[0] // SIDE
    for i in range(SIDE):
        total = own_tile[i * quads : (i + 1) * quads].astype(F32)
        for k in range(SIDE - 1):
            total += first_in[k, i * quads : (i + 1) * quads].astype(F32)
        stacked[:, i * LANES : (i + 1) * LANES] = total.reshape(quads * 8, LANES).astype(BF16)
    packed = jnp.dot(stacked[...], perm[...], preferred_element_type=F32)
    for q in range(SIDE):
        second_send[q] = packed[:, q * LANES : (q + 1) * LANES].astype(BF16)
    second = []
    for k in (2, 1, 3):
        copy = remote(
            second_send.at[(i2 + k) % SIDE],
            second_in.at[k - 1],
            second_send_sem.at[k - 1],
            second_recv_sem.at[k - 1],
            second_peer(k),
        )
        copy.start()
        second.append(copy)
    total = second_send[i2].astype(F32)
    for copy in second:
        copy.wait_recv()
    for k in range(SIDE - 1):
        total += second_in[k].astype(F32)
    spread = jnp.dot(total.astype(BF16), rep[...], preferred_element_type=F32)
    for i in range(SIDE):
        table[i * quads : (i + 1) * quads] = spread[:, i * LANES : (i + 1) * LANES].reshape(quads, 8, LANES)

    lane = lax.broadcasted_iota(jnp.int32, (8, LANES), 1) // PART

    def pick(o, carry):
        held = count_ref[o]
        value = jnp.zeros((8, LANES), F32)
        for s in range(SIDE):
            at = jnp.where(s < held, slot_ref[o, s], SIDE * quads)
            value = jnp.where(lane == s, table[at], value)
        message[o] = value.astype(BF16)
        return carry

    lax.fori_loop(0, n_fsdp, pick, 0)

    mine = i1 * SIDE + i2
    keep = pltpu.make_async_copy(message.at[owner], gathered.at[mine, z, core], swap_recv_sem)
    keep.start()

    def swap(n, carry):
        to = (owner + n + 1) % n_fsdp
        remote(message.at[to], gathered.at[mine, z, core], swap_send_sem, swap_recv_sem, (dp, to)).start()
        return carry

    lax.fori_loop(0, n_fsdp - 1, swap, 0)
    pltpu.make_async_copy(message, message, swap_recv_sem).wait()

    gathers = []
    axes = ((gx, gy, x_peer, y_peer), (gy, gx, y_peer, x_peer))
    for parity, (j1, j2, one, two) in enumerate(axes):
        for k in (2, 1, 3):
            part = gathered.at[j1 * SIDE + j2, :, parity]
            copy = remote(part, part, a_send_sem.at[parity, k - 1], a_recv_sem.at[parity, k - 1], one(k))
            copy.start()
            gathers.append(copy)
        for k in (2, 1, 3):
            part = gathered.at[j1 * SIDE + j2, :, parity]
            copy = remote(part, part, b_send_sem.at[parity, 0, k - 1], b_recv_sem.at[parity, 0, k - 1], two(k))
            copy.start()
            gathers.append(copy)
    late = []
    for k in (1, 3, 2):
        for parity, (j1, j2, one, two) in enumerate(axes):
            part = gathered.at[((j1 + SIDE - k) % SIDE) * SIDE + j2, :, parity]
            remote(part, part, a_send_sem.at[parity, k - 1], a_recv_sem.at[parity, k - 1], one(k)).wait_recv()
            for m in (2, 1, 3):
                copy = remote(part, part, b_send_sem.at[parity, k, m - 1], b_recv_sem.at[parity, k, m - 1], two(m))
                copy.start()
                late.append(copy)
    for parity in range(2):
        for m in range(1, SIDE):
            for k in range(SIDE):
                part = gathered.at[0, :, parity]
                remote(part, part, b_send_sem.at[parity, k, m - 1], b_recv_sem.at[parity, k, m - 1], y_peer(m)).wait_recv()

    for load in loads:
        load.wait()
    order = n_z * 16
    rows = lo_v.shape[1]
    own_rows = pl.ds(2 * dp, 2)

    def piece(p):
        return gathered[p].reshape(order, LANES)

    stack = SIDE * rows
    lhs_v[0:stack] = lr_v[...].reshape(stack, order)
    lhs_v[stack : 2 * stack] = piece(dp).T
    blockdiag = (
        lax.broadcasted_iota(jnp.int32, (stack, LANES), 0) // rows
        == lax.broadcasted_iota(jnp.int32, (stack, LANES), 1) // PART
    )
    lane_part = lax.broadcasted_iota(jnp.int32, (rows, LANES), 1) // PART
    held = count_ref[owner]

    def settle(value, s):
        result = jnp.zeros((rows, LANES), F32)
        for q in range(SIDE):
            block = value[q]
            shift = ((q - s) * PART) % LANES
            if shift:
                block = pltpu.roll(block, shift, axis=1)
            result = jnp.where(lane_part == q, block, result)
        return result

    def column(ct, left_sum):
        pieces = [piece(ct * SIDE + q) for q in range(SIDE)]
        wide = jnp.concatenate(pieces, axis=1)
        both = jnp.dot(lhs_v[...], wide, preferred_element_type=F32)
        mine_rows = [gathered[ct * SIDE + q, own_rows].reshape(rows, LANES) for q in range(SIDE)]
        masked = jnp.concatenate(
            [jnp.where(blockdiag, jnp.concatenate([m.astype(F32)] * SIDE, axis=0), 0.0).astype(BF16) for m in mine_rows],
            axis=1,
        )
        left_sum += lax.dot_general(masked, wide, (((1,), (1,)), ((), ())), preferred_element_type=F32)
        for s in range(SIDE):
            at = slice(s * rows, (s + 1) * rows)
            half_v[ct, at] = settle([both[at, q * LANES : (q + 1) * LANES] for q in range(SIDE)], s).astype(BF16)
            low = slice(stack + s * rows, stack + (s + 1) * rows)
            term_v[ct, at] = settle([both[low, q * LANES : (q + 1) * LANES] for q in range(SIDE)], s)
            own_v[ct, at] = settle([m.astype(F32) for m in mine_rows], s)
        return left_sum

    left_sum = lax.fori_loop(0, SIDE, column, jnp.zeros((stack, order), F32))

    squares = []
    adams = []
    for s in range(SIDE):
        at = slice(s * rows, (s + 1) * rows)
        live = jnp.full((rows, LANES), s, jnp.int32) < jnp.full((rows, LANES), held, jnp.int32)
        precond = jnp.zeros((rows, order), F32)
        for ct in range(SIDE):
            precond += jnp.dot(
                half_v[ct, at], rr_v[s, ct * LANES : (ct + 1) * LANES, :], preferred_element_type=F32
            )
        update_v[s] = precond
        square = precond * precond
        lanes_sum = jnp.zeros((rows, LANES), F32)
        adam_sum = jnp.zeros((rows, LANES), F32)
        for ct in range(SIDE):
            here = slice(ct * LANES, (ct + 1) * LANES)
            lanes_sum += square[:, here]
            value = own_v[ct, at]
            old = mo_v[s, :, here]
            new = jnp.where(live, ADAM_BETA * old + (1.0 - ADAM_BETA) * value * value, old)
            moment_v[s, :, here] = new
            adam = value / (jnp.sqrt(new) + EPSILON)
            adam_sum += adam * adam
            old = lo_v[s, :, here]
            left_v[s, :, here] = jnp.where(
                live, SHAMPOO_BETA * old + (1.0 - SHAMPOO_BETA) * left_sum[at, here], old
            )
            old = ro_v[s, :, here]
            right_v[s, :, here] = jnp.where(
                live, SHAMPOO_BETA * old + (1.0 - SHAMPOO_BETA) * term_v[ct, at], old
            )
        squares.append(jnp.sum(lanes_sum, axis=0, keepdims=True))
        adams.append(jnp.sum(adam_sum, axis=0, keepdims=True))
    norms = jnp.concatenate(squares + adams, axis=0)
    norm_out[...] = norms

    n_dp = SIDE * SIDE

    def share(n, carry):
        to = ((dp + n + 1) % n_dp, owner)
        remote(norm_out, norm_in.at[n], norm_send_sem, norm_recv_sem, to).start()
        return carry

    lax.fori_loop(0, n_dp - 1, share, 0)
    outs = [
        pltpu.make_async_copy(src, dst.at[0], out_sem.at[n])
        for n, (src, dst) in enumerate(((left_v, left_out), (right_v, right_out), (moment_v, moment_out)))
    ]
    for copy in outs:
        copy.start()
    pltpu.make_async_copy(norm_in, norm_in, norm_recv_sem).wait()
    for n in range(n_dp - 1):
        norms += norm_in[n]
    sums = jnp.broadcast_to(jnp.sum(norms, axis=1, keepdims=True), (8, LANES))
    slot = lax.broadcasted_iota(jnp.int32, (SIDE, LANES), 0)
    live = slot < jnp.full((SIDE, LANES), held, jnp.int32)
    scale = jnp.where(live, jnp.sqrt(sums[SIDE:] / jnp.where(live, sums[:SIDE], 1.0)), 0.0)
    for s in range(SIDE):
        wide = jnp.broadcast_to(jnp.concatenate([scale[s : s + 1]] * SIDE, axis=1), (rows, order))
        update_v[s] = update_v[s] * wide
    last = pltpu.make_async_copy(update_v, update_out.at[0], out_sem.at[3])
    last.start()
    for copy in first + second + gathers + late:
        copy.wait_send()
    pltpu.make_async_copy(
        message.at[pl.ds(0, n_fsdp - 1)], message.at[pl.ds(0, n_fsdp - 1)], swap_send_sem
    ).wait()
    pltpu.make_async_copy(norm_in, norm_in, norm_send_sem).wait()
    for copy in outs + [last]:
        copy.wait()


def on_device(
    grads, left_stats, right_stats, left_root, right_root, second_moment, slot_block, counts
):
    n_fsdp = lax.axis_size("fsdp")
    n_z = n_fsdp // 2
    blocks, slab = grads.shape[1:3]
    slots, rows, order = left_stats.shape[1:]
    quads = blocks // SIDE
    stack = slots * rows
    blocks = blocks
    hbm = pl.BlockSpec(memory_space=pl.ANY)
    smem = pl.BlockSpec(memory_space=pltpu.SMEM)
    out = jax.ShapeDtypeStruct(left_stats.shape, F32)
    dma = pltpu.SemaphoreType.DMA
    vmem = pltpu.VMEM
    n_dp = SIDE * SIDE
    import functools

    return tuple(
        pl.pallas_call(
            functools.partial(kernel, n_fsdp),
            out_shape=(out,) * 4,
            in_specs=[smem, smem] + [hbm] * 6,
            out_specs=(hbm,) * 4,
            scratch_shapes=[
                vmem((blocks, slab, LANES), BF16),
                vmem((SIDE - 1, blocks, slab, LANES), BF16),
                vmem((quads * slab, SIDE * LANES), BF16),
                vmem((SIDE * LANES, SIDE * LANES), BF16),
                vmem((LANES, SIDE * LANES), BF16),
                vmem((SIDE, quads * slab, LANES), BF16),
                vmem((SIDE - 1, quads * slab, LANES), BF16),
                vmem((blocks + 1, slab, LANES), F32),
                vmem((n_fsdp, slab, LANES), BF16),
                vmem((n_dp, n_z, 2, slab, LANES), BF16),
                vmem((slots, rows, order), F32),
                vmem((slots, rows, order), F32),
                vmem((slots, rows, order), BF16),
                vmem((slots, order, order), BF16),
                vmem((slots, rows, order), F32),
                vmem((slots, rows, order), F32),
                vmem((slots, rows, order), F32),
                vmem((slots, rows, order), F32),
                vmem((slots, rows, order), F32),
                vmem((2 * stack, order), BF16),
                vmem((SIDE, stack, LANES), BF16),
                vmem((SIDE, stack, LANES), F32),
                vmem((SIDE, stack, LANES), F32),
                vmem((8, LANES), F32),
                vmem((n_dp - 1, 8, LANES), F32),
                dma((6,)),
                dma((4,)),
                dma((SIDE - 1,)),
                dma((SIDE - 1,)),
                dma((SIDE - 1,)),
                dma((SIDE - 1,)),
                dma,
                dma,
                dma((2, SIDE - 1)),
                dma((2, SIDE - 1)),
                dma((2, SIDE, SIDE - 1)),
                dma((2, SIDE, SIDE - 1)),
                dma,
                dma,
                pltpu.SemaphoreType.REGULAR,
                pltpu.SemaphoreType.REGULAR,
            ],
            compiler_params=pltpu.CompilerParams(
                collective_id=0, has_side_effects=True, vmem_limit_bytes=48 << 20
            ),
            name="shampoo",
        )(slot_block, counts, grads, left_stats, right_stats, left_root, right_root, second_moment)
    )


def solution(mesh):
    in_specs = (
        P("dp", None, "fsdp", None),
        P("fsdp", None, "dp", None),
        P("fsdp", None, "dp", None),
        P("fsdp", None, "dp", None),
        P("fsdp", None, None, None),
        P("fsdp", None, "dp", None),
        P(),
        P(),
    )
    out_specs = (
        P("fsdp", None, "dp", None),
        P("fsdp", None, "dp", None),
        P("fsdp", None, "dp", None),
        P("fsdp", None, "dp", None),
    )
    return jax.shard_map(
        on_device, mesh=mesh, in_specs=in_specs, out_specs=out_specs, check_vma=False
    )
```

```python
import jax
import jax.numpy as jnp
from jax import lax
from jax.experimental import pallas as pl
from jax.experimental.pallas import tpu as pltpu
from jax.sharding import PartitionSpec as P

SHAMPOO_BETA = 0.998
ADAM_BETA = 0.95
EPSILON = 1e-08

SIDE = 4
LANES = 128
ZONE = 8
PART = LANES // SIDE
F32 = jnp.float32
BF16 = jnp.bfloat16


def kernel(
    n_fsdp,
    slot_ref,
    count_ref,
    grads,
    left_old,
    right_old,
    left_root,
    right_root,
    moment_old,
    left_out,
    right_out,
    moment_out,
    update_out,
    own_tile,
    first_in,
    stacked,
    perm,
    rep,
    second_send,
    second_in,
    table,
    message,
    gathered,
    lo_v,
    ro_v,
    lr_v,
    rr_v,
    mo_v,
    left_v,
    right_v,
    moment_v,
    update_v,
    lhs_v,
    half_v,
    term_v,
    own_v,
    norm_out,
    norm_in,
    load_sem,
    out_sem,
    first_send_sem,
    first_recv_sem,
    second_send_sem,
    second_recv_sem,
    swap_send_sem,
    swap_recv_sem,
    a_send_sem,
    a_recv_sem,
    b_send_sem,
    b_recv_sem,
    norm_send_sem,
    norm_recv_sem,
    met,
):
    dp = lax.axis_index("dp")
    owner = lax.axis_index("fsdp")
    gx, gy = dp // SIDE, dp % SIDE
    z, core = owner // 2, owner % 2
    n_z = n_fsdp // 2
    other = 1 - core
    i1 = gx * other + gy * core
    i2 = gy * other + gx * core

    def first_peer(k):
        return (((gx + k * other) % SIDE) * SIDE + (gy + k * core) % SIDE, owner)

    def second_peer(k):
        return (((gx + k * core) % SIDE) * SIDE + (gy + k * other) % SIDE, owner)

    def x_peer(k):
        return (((gx + k) % SIDE) * SIDE + gy, owner)

    def y_peer(k):
        return (gx * SIDE + (gy + k) % SIDE, owner)

    def z_peer(k):
        return (dp, ((z + k + n_z) % n_z) * 2 + core)

    def remote(src, dst, send, recv, peer):
        return pltpu.make_async_remote_copy(
            src_ref=src,
            dst_ref=dst,
            send_sem=send,
            recv_sem=recv,
            device_id=peer,
            device_id_type=pl.DeviceIdType.MESH,
        )

    own_load = pltpu.make_async_copy(
        grads.at[0, :, :, pl.ds(pl.multiple_of(i1 * LANES, LANES), LANES)], own_tile, load_sem.at[0]
    )
    own_load.start()

    barrier = pltpu.get_barrier_semaphore()
    greeted = [x_peer(k) for k in range(1, SIDE)] + [y_peer(k) for k in range(1, SIDE)]
    for k in (0, 1, -1, 2, -2):
        for c in (core, other):
            if k or c is other:
                greeted.append((dp, ((z + k + n_z) % n_z) * 2 + c))
    for peer in greeted:
        pl.semaphore_signal(barrier, inc=1, device_id=peer, device_id_type=pl.DeviceIdType.MESH)
    loads = [
        pltpu.make_async_copy(src.at[0], dst, load_sem.at[1 + n])
        for n, (src, dst) in enumerate(
            ((left_old, lo_v), (right_old, ro_v), (left_root, lr_v), (right_root, rr_v), (moment_old, mo_v))
        )
    ]
    for load in loads:
        load.start()
    pl.semaphore_wait(barrier, len(greeted))

    first = []
    for k in (2, 1, 3):
        tile = pl.ds(pl.multiple_of(((i1 + k) % SIDE) * LANES, LANES), LANES)
        copy = remote(
            grads.at[0, :, :, tile],
            first_in.at[k - 1],
            first_send_sem.at[k - 1],
            first_recv_sem.at[k - 1],
            first_peer(k),
        )
        copy.start()
        first.append(copy)

    row = lax.broadcasted_iota(jnp.int32, (SIDE * LANES, SIDE * LANES), 0)
    col = lax.broadcasted_iota(jnp.int32, (SIDE * LANES, SIDE * LANES), 1)
    want = ((col % LANES) // PART) * LANES + (col // LANES) * PART + col % PART
    perm[...] = jnp.where(row == want, 1.0, 0.0).astype(BF16)
    row = lax.broadcasted_iota(jnp.int32, (LANES, SIDE * LANES), 0)
    col = lax.broadcasted_iota(jnp.int32, (LANES, SIDE * LANES), 1)
    rep[...] = jnp.where(row == (col // LANES) * PART + col % PART, 1.0, 0.0).astype(BF16)
    table[pl.ds(SIDE * 32, 1)] = jnp.zeros((1, 8, LANES), F32)

    reach = []
    k = 2
    while k < n_z // 2:
        reach.append(k)
        k *= 2

    def tell(n):
        for k in (reach[n], -reach[n]):
            pl.semaphore_signal(
                met.at[n], inc=1, device_id=z_peer(k), device_id_type=pl.DeviceIdType.MESH
            )

    tell(0)
    for n in range(1, len(reach)):
        pl.semaphore_wait(met.at[n - 1], 2)
        tell(n)

    own_load.wait()
    for copy in first:
        copy.wait_recv()
    quads = own_tile.shape[0] // SIDE
    for i in range(SIDE):
        total = own_tile[i * quads : (i + 1) * quads].astype(F32)
        for k in range(SIDE - 1):
            total += first_in[k, i * quads : (i + 1) * quads].astype(F32)
        stacked[:, i * LANES : (i + 1) * LANES] = total.reshape(quads * 8, LANES).astype(BF16)
    packed = jnp.dot(stacked[...], perm[...], preferred_element_type=F32)
    for q in range(SIDE):
        second_send[q] = packed[:, q * LANES : (q + 1) * LANES].astype(BF16)
    second = []
    for k in (2, 1, 3):
        copy = remote(
            second_send.at[(i2 + k) % SIDE],
            second_in.at[k - 1],
            second_send_sem.at[k - 1],
            second_recv_sem.at[k - 1],
            second_peer(k),
        )
        copy.start()
        second.append(copy)
    total = second_send[i2].astype(F32)
    for copy in second:
        copy.wait_recv()
    for k in range(SIDE - 1):
        total += second_in[k].astype(F32)
    spread = jnp.dot(total.astype(BF16), rep[...], preferred_element_type=F32)
    for i in range(SIDE):
        table[i * quads : (i + 1) * quads] = spread[:, i * LANES : (i + 1) * LANES].reshape(quads, 8, LANES)

    lane = lax.broadcasted_iota(jnp.int32, (8, LANES), 1) // PART

    def pick(o, carry):
        held = count_ref[o]
        value = jnp.zeros((8, LANES), F32)
        for s in range(SIDE):
            at = jnp.where(s < held, slot_ref[o, s], SIDE * quads)
            value = jnp.where(lane == s, table[at], value)
        message[o] = value.astype(BF16)
        return carry

    lax.fori_loop(0, n_fsdp, pick, 0)

    pl.semaphore_wait(met.at[len(reach) - 1], 2)
    mine = i1 * SIDE + i2
    zone = z // ZONE
    keep = pltpu.make_async_copy(message.at[owner], gathered.at[mine, z, core], swap_recv_sem.at[zone])
    keep.start()

    def send_to(to):
        remote(
            message.at[to], gathered.at[mine, z, core], swap_send_sem, swap_recv_sem.at[zone], (dp, to)
        ).start()

    send_to(z * 2 + other)

    def swap(n, carry):
        for step in (n + 1, n_z - 1 - n):
            for c in range(2):
                send_to(((z + step) % n_z) * 2 + c)
        return carry

    lax.fori_loop(0, n_z // 2 - 1, swap, 0)
    for c in range(2):
        send_to(((z + n_z // 2) % n_z) * 2 + c)

    axes = ((gx, gy, x_peer, y_peer), (gy, gx, y_peer, x_peer))
    zones = n_z // ZONE

    def along(parity, n, k, m, j1_back):
        j1, j2, one, two = axes[parity]
        at = pl.ds(pl.multiple_of(((zone + near_first[n]) % zones) * ZONE, ZONE), ZONE)
        part = gathered.at[((j1 + SIDE - j1_back) % SIDE) * SIDE + j2, at, parity]
        if m:
            return remote(part, part, b_send_sem, b_recv_sem, two(m))
        return remote(part, part, a_send_sem, a_recv_sem.at[n, parity, k - 1], one(k))

    near_first = (0, 1, zones - 1, 2)

    def first_gather(n):
        here = (zone + near_first[n]) % zones
        whole = message.at[pl.ds(0, 2 * ZONE)]
        pltpu.make_async_copy(whole, whole, swap_recv_sem.at[here]).wait()
        for k in (2, 1, 3):
            for parity in range(2):
                along(parity, n, k, 0, 0).start()
        for m in (2, 1, 3):
            for parity in range(2):
                along(parity, n, 0, m, 0).start()

    def second_gather(n):
        for k in (1, 3, 2):
            for parity in range(2):
                along(parity, n, k, 0, k).wait_recv()
                for m in (2, 1, 3):
                    along(parity, n, k, m, k).start()

    for n in range(zones):
        first_gather(n)
        if n:
            second_gather(n - 1)
    second_gather(zones - 1)
    third = gathered.at[pl.ds(0, SIDE * (SIDE - 1))]
    pltpu.make_async_copy(third, third, b_recv_sem).wait()

    for load in loads:
        load.wait()
    order = n_z * 16
    rows = lo_v.shape[1]
    own_rows = pl.ds(2 * dp, 2)

    def piece(p):
        return gathered[p].reshape(order, LANES)

    stack = SIDE * rows
    lhs_v[0:stack] = lr_v[...].reshape(stack, order)
    lhs_v[stack : 2 * stack] = piece(dp).T
    blockdiag = (
        lax.broadcasted_iota(jnp.int32, (stack, LANES), 0) // rows
        == lax.broadcasted_iota(jnp.int32, (stack, LANES), 1) // PART
    )
    lane_part = lax.broadcasted_iota(jnp.int32, (rows, LANES), 1) // PART
    held = count_ref[owner]

    def settle(value, s):
        result = jnp.zeros((rows, LANES), F32)
        for q in range(SIDE):
            block = value[q]
            shift = ((q - s) * PART) % LANES
            if shift:
                block = pltpu.roll(block, shift, axis=1)
            result = jnp.where(lane_part == q, block, result)
        return result

    def column(ct, left_sum):
        pieces = [piece(ct * SIDE + q) for q in range(SIDE)]
        wide = jnp.concatenate(pieces, axis=1)
        both = jnp.dot(lhs_v[...], wide, preferred_element_type=F32)
        mine_rows = [gathered[ct * SIDE + q, own_rows].reshape(rows, LANES) for q in range(SIDE)]
        masked = jnp.concatenate(
            [jnp.where(blockdiag, jnp.concatenate([m.astype(F32)] * SIDE, axis=0), 0.0).astype(BF16) for m in mine_rows],
            axis=1,
        )
        left_sum += lax.dot_general(masked, wide, (((1,), (1,)), ((), ())), preferred_element_type=F32)
        for s in range(SIDE):
            at = slice(s * rows, (s + 1) * rows)
            half_v[ct, at] = settle([both[at, q * LANES : (q + 1) * LANES] for q in range(SIDE)], s).astype(BF16)
            low = slice(stack + s * rows, stack + (s + 1) * rows)
            term_v[ct, at] = settle([both[low, q * LANES : (q + 1) * LANES] for q in range(SIDE)], s)
            own_v[ct, at] = settle([m.astype(F32) for m in mine_rows], s)
        return left_sum

    left_sum = lax.fori_loop(0, SIDE, column, jnp.zeros((stack, order), F32))
    for s in range(SIDE):
        left_v[s] = left_sum[s * rows : (s + 1) * rows]

    squares = []
    adams = []
    for s in range(SIDE):
        at = slice(s * rows, (s + 1) * rows)
        live = jnp.full((rows, LANES), s, jnp.int32) < jnp.full((rows, LANES), held, jnp.int32)
        precond = jnp.zeros((rows, order), F32)
        for ct in range(SIDE):
            precond += jnp.dot(
                half_v[ct, at], rr_v[s, ct * LANES : (ct + 1) * LANES, :], preferred_element_type=F32
            )
        update_v[s] = precond
        square = precond * precond
        lanes_sum = jnp.zeros((rows, LANES), F32)
        adam_sum = jnp.zeros((rows, LANES), F32)
        for ct in range(SIDE):
            here = slice(ct * LANES, (ct + 1) * LANES)
            lanes_sum += square[:, here]
            value = own_v[ct, at]
            old = mo_v[s, :, here]
            new = jnp.where(live, ADAM_BETA * old + (1.0 - ADAM_BETA) * value * value, old)
            moment_v[s, :, here] = new
            adam = value / (jnp.sqrt(new) + EPSILON)
            adam_sum += adam * adam
        squares.append(jnp.sum(lanes_sum, axis=0, keepdims=True))
        adams.append(jnp.sum(adam_sum, axis=0, keepdims=True))
    norms = jnp.concatenate(squares + adams, axis=0)
    norm_out[...] = norms

    n_dp = SIDE * SIDE

    def share(n, carry):
        to = ((dp + n + 1) % n_dp, owner)
        remote(norm_out, norm_in.at[n], norm_send_sem, norm_recv_sem, to).start()
        return carry

    lax.fori_loop(0, n_dp - 1, share, 0)
    for s in range(SIDE):
        at = slice(s * rows, (s + 1) * rows)
        live = jnp.full((rows, LANES), s, jnp.int32) < jnp.full((rows, LANES), held, jnp.int32)
        for ct in range(SIDE):
            here = slice(ct * LANES, (ct + 1) * LANES)
            old = lo_v[s, :, here]
            left_v[s, :, here] = jnp.where(
                live, SHAMPOO_BETA * old + (1.0 - SHAMPOO_BETA) * left_v[s, :, here], old
            )
            old = ro_v[s, :, here]
            right_v[s, :, here] = jnp.where(
                live, SHAMPOO_BETA * old + (1.0 - SHAMPOO_BETA) * term_v[ct, at], old
            )
    outs = [
        pltpu.make_async_copy(src, dst.at[0], out_sem.at[n])
        for n, (src, dst) in enumerate(((left_v, left_out), (right_v, right_out), (moment_v, moment_out)))
    ]
    for copy in outs:
        copy.start()
    pltpu.make_async_copy(norm_in, norm_in, norm_recv_sem).wait()
    for n in range(n_dp - 1):
        norms += norm_in[n]
    sums = jnp.broadcast_to(jnp.sum(norms, axis=1, keepdims=True), (8, LANES))
    slot = lax.broadcasted_iota(jnp.int32, (SIDE, LANES), 0)
    live = slot < jnp.full((SIDE, LANES), held, jnp.int32)
    scale = jnp.where(live, jnp.sqrt(sums[SIDE:] / jnp.where(live, sums[:SIDE], 1.0)), 0.0)
    for s in range(SIDE):
        wide = jnp.broadcast_to(jnp.concatenate([scale[s : s + 1]] * SIDE, axis=1), (rows, order))
        update_v[s] = update_v[s] * wide
    last = pltpu.make_async_copy(update_v, update_out.at[0], out_sem.at[3])
    last.start()
    for copy in first + second:
        copy.wait_send()
    sent = gathered.at[pl.ds(0, SIDE - 1)]
    pltpu.make_async_copy(sent, sent, a_send_sem).wait()
    pltpu.make_async_copy(third, third, b_send_sem).wait()
    pltpu.make_async_copy(
        message.at[pl.ds(0, n_fsdp - 1)], message.at[pl.ds(0, n_fsdp - 1)], swap_send_sem
    ).wait()
    pltpu.make_async_copy(norm_in, norm_in, norm_send_sem).wait()
    for copy in outs + [last]:
        copy.wait()


def on_device(
    grads, left_stats, right_stats, left_root, right_root, second_moment, slot_block, counts
):
    n_fsdp = lax.axis_size("fsdp")
    n_z = n_fsdp // 2
    blocks, slab = grads.shape[1:3]
    slots, rows, order = left_stats.shape[1:]
    quads = blocks // SIDE
    stack = slots * rows
    blocks = blocks
    hbm = pl.BlockSpec(memory_space=pl.ANY)
    smem = pl.BlockSpec(memory_space=pltpu.SMEM)
    out = jax.ShapeDtypeStruct(left_stats.shape, F32)
    dma = pltpu.SemaphoreType.DMA
    vmem = pltpu.VMEM
    n_dp = SIDE * SIDE
    import functools

    return tuple(
        pl.pallas_call(
            functools.partial(kernel, n_fsdp),
            out_shape=(out,) * 4,
            in_specs=[smem, smem] + [hbm] * 6,
            out_specs=(hbm,) * 4,
            scratch_shapes=[
                vmem((blocks, slab, LANES), BF16),
                vmem((SIDE - 1, blocks, slab, LANES), BF16),
                vmem((quads * slab, SIDE * LANES), BF16),
                vmem((SIDE * LANES, SIDE * LANES), BF16),
                vmem((LANES, SIDE * LANES), BF16),
                vmem((SIDE, quads * slab, LANES), BF16),
                vmem((SIDE - 1, quads * slab, LANES), BF16),
                vmem((blocks + 1, slab, LANES), F32),
                vmem((n_fsdp, slab, LANES), BF16),
                vmem((n_dp, n_z, 2, slab, LANES), BF16),
                vmem((slots, rows, order), F32),
                vmem((slots, rows, order), F32),
                vmem((slots, rows, order), BF16),
                vmem((slots, order, order), BF16),
                vmem((slots, rows, order), F32),
                vmem((slots, rows, order), F32),
                vmem((slots, rows, order), F32),
                vmem((slots, rows, order), F32),
                vmem((slots, rows, order), F32),
                vmem((2 * stack, order), BF16),
                vmem((SIDE, stack, LANES), BF16),
                vmem((SIDE, stack, LANES), F32),
                vmem((SIDE, stack, LANES), F32),
                vmem((8, LANES), F32),
                vmem((n_dp - 1, 8, LANES), F32),
                dma((6,)),
                dma((4,)),
                dma((SIDE - 1,)),
                dma((SIDE - 1,)),
                dma((SIDE - 1,)),
                dma((SIDE - 1,)),
                dma,
                dma((n_z // ZONE,)),
                dma,
                dma((n_z // ZONE, 2, SIDE - 1)),
                dma,
                dma,
                dma,
                dma,
                pltpu.SemaphoreType.REGULAR((4,)),
            ],
            compiler_params=pltpu.CompilerParams(
                collective_id=0, has_side_effects=True, vmem_limit_bytes=67043328
            ),
            name="shampoo",
        )(slot_block, counts, grads, left_stats, right_stats, left_root, right_root, second_moment)
    )


def solution(mesh):
    in_specs = (
        P("dp", None, "fsdp", None),
        P("fsdp", None, "dp", None),
        P("fsdp", None, "dp", None),
        P("fsdp", None, "dp", None),
        P("fsdp", None, None, None),
        P("fsdp", None, "dp", None),
        P(),
        P(),
    )
    out_specs = (
        P("fsdp", None, "dp", None),
        P("fsdp", None, "dp", None),
        P("fsdp", None, "dp", None),
        P("fsdp", None, "dp", None),
    )
    return jax.shard_map(
        on_device, mesh=mesh, in_specs=in_specs, out_specs=out_specs, check_vma=False
    )
```

```python
import functools

import jax
import jax.numpy as jnp
from jax import lax
from jax.experimental import pallas as pl
from jax.experimental.pallas import tpu as pltpu
from jax.sharding import PartitionSpec as P

SHAMPOO_BETA = 0.998
ADAM_BETA = 0.95
EPSILON = 1e-08

SIDE = 4
LANES = 128
SPAN = 4
PART = LANES // SIDE
F32 = jnp.float32
BF16 = jnp.bfloat16


def kernel(
    n_fsdp,
    span,
    slot_ref,
    count_ref,
    grads,
    left_old,
    right_old,
    left_root,
    right_root,
    moment_old,
    left_out,
    right_out,
    moment_out,
    update_out,
    scale_out,
    own_tile,
    first_in,
    stacked,
    perm,
    rep,
    second_send,
    second_in,
    table,
    message,
    gathered,
    lo_v,
    ro_v,
    lr_v,
    rr_v,
    mo_v,
    left_v,
    right_v,
    moment_v,
    update_v,
    lhs_v,
    half_v,
    term_v,
    own_v,
    norm_out,
    norm_in,
    scale_v,
    load_sem,
    out_sem,
    first_send_sem,
    first_recv_sem,
    second_send_sem,
    second_recv_sem,
    swap_send_sem,
    swap_recv_sem,
    a_send_sem,
    a_recv_sem,
    b_send_sem,
    b_recv_sem,
    norm_send_sem,
    norm_recv_sem,
    met,
):
    dp = lax.axis_index("dp")
    owner = lax.axis_index("fsdp")
    gx, gy = dp // SIDE, dp % SIDE
    z, core = owner // 2, owner % 2
    n_z = n_fsdp // 2
    other = 1 - core
    i1 = gx * other + gy * core
    i2 = gy * other + gx * core

    def first_peer(k):
        return (((gx + k * other) % SIDE) * SIDE + (gy + k * core) % SIDE, owner)

    def second_peer(k):
        return (((gx + k * core) % SIDE) * SIDE + (gy + k * other) % SIDE, owner)

    def x_peer(k):
        return (((gx + k) % SIDE) * SIDE + gy, owner)

    def y_peer(k):
        return (gx * SIDE + (gy + k) % SIDE, owner)

    def z_peer(k):
        return (dp, ((z + k + n_z) % n_z) * 2 + core)

    def remote(src, dst, send, recv, peer):
        return pltpu.make_async_remote_copy(
            src_ref=src,
            dst_ref=dst,
            send_sem=send,
            recv_sem=recv,
            device_id=peer,
            device_id_type=pl.DeviceIdType.MESH,
        )

    own_load = pltpu.make_async_copy(
        grads.at[0, :, :, pl.ds(pl.multiple_of(i1 * LANES, LANES), LANES)], own_tile, load_sem.at[0]
    )
    own_load.start()

    barrier = pltpu.get_barrier_semaphore()
    greeted = [x_peer(k) for k in range(1, SIDE)] + [y_peer(k) for k in range(1, SIDE)]
    for k in (0, 1, -1, 2, -2):
        for c in (core, other):
            if k or c is other:
                greeted.append((dp, ((z + k + n_z) % n_z) * 2 + c))
    for peer in greeted:
        pl.semaphore_signal(barrier, inc=1, device_id=peer, device_id_type=pl.DeviceIdType.MESH)
    loads = [
        pltpu.make_async_copy(src.at[0], dst, load_sem.at[1 + n])
        for n, (src, dst) in enumerate(
            ((left_old, lo_v), (right_old, ro_v), (left_root, lr_v), (right_root, rr_v), (moment_old, mo_v))
        )
    ]
    for load in loads:
        load.start()
    pl.semaphore_wait(barrier, len(greeted))

    first = []
    for k in (2, 1, 3):
        tile = pl.ds(pl.multiple_of(((i1 + k) % SIDE) * LANES, LANES), LANES)
        copy = remote(
            grads.at[0, :, :, tile],
            first_in.at[k - 1],
            first_send_sem.at[k - 1],
            first_recv_sem.at[k - 1],
            first_peer(k),
        )
        copy.start()
        first.append(copy)

    row = lax.broadcasted_iota(jnp.int32, (SIDE * LANES, SIDE * LANES), 0)
    col = lax.broadcasted_iota(jnp.int32, (SIDE * LANES, SIDE * LANES), 1)
    want = ((col % LANES) // PART) * LANES + (col // LANES) * PART + col % PART
    perm[...] = jnp.where(row == want, 1.0, 0.0).astype(BF16)
    row = lax.broadcasted_iota(jnp.int32, (LANES, SIDE * LANES), 0)
    col = lax.broadcasted_iota(jnp.int32, (LANES, SIDE * LANES), 1)
    rep[...] = jnp.where(row == (col // LANES) * PART + col % PART, 1.0, 0.0).astype(BF16)
    table[pl.ds(SIDE * 32, 1)] = jnp.zeros((1, 8, LANES), F32)

    reach = []
    k = 2
    while k < n_z // 2:
        reach.append(k)
        k *= 2

    def tell(n):
        for k in (reach[n], -reach[n]):
            pl.semaphore_signal(
                met.at[n], inc=1, device_id=z_peer(k), device_id_type=pl.DeviceIdType.MESH
            )

    tell(0)
    for n in range(1, len(reach)):
        pl.semaphore_wait(met.at[n - 1], 2)
        tell(n)

    own_load.wait()
    for copy in first:
        copy.wait_recv()
    quads = own_tile.shape[0] // SIDE
    for i in range(SIDE):
        total = own_tile[i * quads : (i + 1) * quads].astype(F32)
        for k in range(SIDE - 1):
            total += first_in[k, i * quads : (i + 1) * quads].astype(F32)
        stacked[:, i * LANES : (i + 1) * LANES] = total.reshape(quads * 8, LANES).astype(BF16)
    packed = jnp.dot(stacked[...], perm[...], preferred_element_type=F32)
    for q in range(SIDE):
        second_send[q] = packed[:, q * LANES : (q + 1) * LANES].astype(BF16)
    second = []
    for k in (2, 1, 3):
        copy = remote(
            second_send.at[(i2 + k) % SIDE],
            second_in.at[k - 1],
            second_send_sem.at[k - 1],
            second_recv_sem.at[k - 1],
            second_peer(k),
        )
        copy.start()
        second.append(copy)
    total = second_send[i2].astype(F32)
    for copy in second:
        copy.wait_recv()
    for k in range(SIDE - 1):
        total += second_in[k].astype(F32)
    spread = jnp.dot(total.astype(BF16), rep[...], preferred_element_type=F32)
    for i in range(SIDE):
        table[i * quads : (i + 1) * quads] = spread[:, i * LANES : (i + 1) * LANES].reshape(quads, 8, LANES)

    lane = lax.broadcasted_iota(jnp.int32, (8, LANES), 1) // PART

    def pick(o, carry):
        held = count_ref[o]
        value = jnp.zeros((8, LANES), F32)
        for s in range(SIDE):
            at = jnp.where(s < held, slot_ref[s, o], SIDE * quads)
            value = jnp.where(lane == s, table[at], value)
        message[o] = value.astype(BF16)
        return carry

    lax.fori_loop(0, n_fsdp, pick, 0, unroll=4)

    pl.semaphore_wait(met.at[len(reach) - 1], 2)
    mine = i1 * SIDE + i2
    zone = z // span
    keep = pltpu.make_async_copy(message.at[owner], gathered.at[mine, z, core], swap_recv_sem.at[zone])
    keep.start()

    def send_to(to):
        remote(
            message.at[to], gathered.at[mine, z, core], swap_send_sem, swap_recv_sem.at[zone], (dp, to)
        ).start()

    send_to(z * 2 + other)

    def swap(n, carry):
        for step in (n + 1, n_z - 1 - n):
            for c in range(2):
                send_to(((z + step) % n_z) * 2 + c)
        return carry

    lax.fori_loop(0, n_z // 2 - 1, swap, 0, unroll=5)
    for c in range(2):
        send_to(((z + n_z // 2) % n_z) * 2 + c)

    axes = ((gx, gy, x_peer, y_peer), (gy, gx, y_peer, x_peer))
    zones = n_z // span

    def along(parity, n, k, m, j1_back):
        j1, j2, one, two = axes[parity]
        at = pl.ds(pl.multiple_of(((zone + near_first[n]) % zones) * span, span), span)
        part = gathered.at[((j1 + SIDE - j1_back) % SIDE) * SIDE + j2, at, parity]
        if m:
            return remote(part, part, b_send_sem, b_recv_sem, two(m))
        return remote(part, part, a_send_sem, a_recv_sem.at[n, parity, k - 1], one(k))

    near_first = sorted(range(zones), key=lambda n: min(n, zones - n))

    def first_gather(n):
        here = (zone + near_first[n]) % zones
        whole = message.at[pl.ds(0, 2 * span)]
        pltpu.make_async_copy(whole, whole, swap_recv_sem.at[here]).wait()
        for k in (2, 1, 3):
            for parity in range(2):
                along(parity, n, k, 0, 0).start()
        for m in (2, 1, 3):
            for parity in range(2):
                along(parity, n, 0, m, 0).start()

    def second_gather(n):
        for k in (1, 3, 2):
            for parity in range(2):
                along(parity, n, k, 0, k).wait_recv()
                for m in (2, 1, 3):
                    along(parity, n, k, m, k).start()

    for n in range(zones):
        first_gather(n)
        if n:
            second_gather(n - 1)
    second_gather(zones - 1)
    third = gathered.at[pl.ds(0, SIDE * (SIDE - 1))]
    pltpu.make_async_copy(third, third, b_recv_sem).wait()

    for load in loads:
        load.wait()
    order = n_z * 16
    rows = lo_v.shape[1]
    own_rows = pl.ds(2 * dp, 2)

    def piece(p):
        return gathered[p].reshape(order, LANES)

    stack = SIDE * rows
    blockdiag = (
        lax.broadcasted_iota(jnp.int32, (stack, LANES), 0) // rows
        == lax.broadcasted_iota(jnp.int32, (stack, LANES), 1) // PART
    )
    lane_part = lax.broadcasted_iota(jnp.int32, (rows, LANES), 1) // PART
    held = count_ref[owner]

    def settle(value, s):
        result = jnp.zeros((rows, LANES), F32)
        for q in range(SIDE):
            block = value[q]
            shift = ((q - s) * PART) % LANES
            if shift:
                block = pltpu.roll(block, shift, axis=1)
            result = jnp.where(lane_part == q, block, result)
        return result

    def own_part(ct):
        return [gathered[ct * SIDE + q, own_rows].reshape(rows, LANES) for q in range(SIDE)]

    def wide_part(ct):
        return jnp.concatenate([piece(ct * SIDE + q) for q in range(SIDE)], axis=1)

    def halves(ct, carry):
        both = jnp.dot(lr_v[...].reshape(stack, order), wide_part(ct), preferred_element_type=F32)
        mine_rows = own_part(ct)
        for s in range(SIDE):
            at = slice(s * rows, (s + 1) * rows)
            half_v[ct, at] = settle([both[at, q * LANES : (q + 1) * LANES] for q in range(SIDE)], s).astype(BF16)
            own_v[ct, at] = settle([m.astype(F32) for m in mine_rows], s)
        return carry

    lax.fori_loop(0, SIDE, halves, 0)

    def terms(ct, left_sum):
        wide = wide_part(ct)
        both = jnp.dot(lhs_v[...], wide, preferred_element_type=F32)
        masked = jnp.concatenate(
            [
                jnp.where(blockdiag, jnp.concatenate([m.astype(F32)] * SIDE, axis=0), 0.0).astype(BF16)
                for m in own_part(ct)
            ],
            axis=1,
        )
        left_sum += lax.dot_general(masked, wide, (((1,), (1,)), ((), ())), preferred_element_type=F32)
        for s in range(SIDE):
            at = slice(s * rows, (s + 1) * rows)
            term_v[ct, at] = settle([both[at, q * LANES : (q + 1) * LANES] for q in range(SIDE)], s)
        return left_sum

    squares = []
    adams = []
    for s in range(SIDE):
        at = slice(s * rows, (s + 1) * rows)
        live = jnp.full((rows, LANES), s, jnp.int32) < jnp.full((rows, LANES), held, jnp.int32)
        precond = jnp.zeros((rows, order), F32)
        for ct in range(SIDE):
            precond += jnp.dot(
                half_v[ct, at], rr_v[s, ct * LANES : (ct + 1) * LANES, :], preferred_element_type=F32
            )
        update_v[s] = precond
        square = precond * precond
        lanes_sum = jnp.zeros((rows, LANES), F32)
        adam_sum = jnp.zeros((rows, LANES), F32)
        for ct in range(SIDE):
            here = slice(ct * LANES, (ct + 1) * LANES)
            lanes_sum += square[:, here]
            value = own_v[ct, at]
            old = mo_v[s, :, here]
            new = jnp.where(live, ADAM_BETA * old + (1.0 - ADAM_BETA) * value * value, old)
            moment_v[s, :, here] = new
            adam = value / (jnp.sqrt(new) + EPSILON)
            adam_sum += adam * adam
        squares.append(jnp.sum(lanes_sum, axis=0, keepdims=True))
        adams.append(jnp.sum(adam_sum, axis=0, keepdims=True))
    norms = jnp.concatenate(squares + adams, axis=0)
    norm_out[...] = norms

    n_dp = SIDE * SIDE

    def share(n, carry):
        to = ((dp + n + 1) % n_dp, owner)
        remote(norm_out, norm_in.at[n], norm_send_sem, norm_recv_sem, to).start()
        return carry

    lax.fori_loop(0, n_dp - 1, share, 0)
    lhs_v[...] = piece(dp).T
    left_sum = lax.fori_loop(0, SIDE, terms, jnp.zeros((stack, order), F32))
    for s in range(SIDE):
        at = slice(s * rows, (s + 1) * rows)
        live = jnp.full((rows, LANES), s, jnp.int32) < jnp.full((rows, LANES), held, jnp.int32)
        for ct in range(SIDE):
            here = slice(ct * LANES, (ct + 1) * LANES)
            old = lo_v[s, :, here]
            left_v[s, :, here] = jnp.where(
                live, SHAMPOO_BETA * old + (1.0 - SHAMPOO_BETA) * left_sum[at, here], old
            )
            old = ro_v[s, :, here]
            right_v[s, :, here] = jnp.where(
                live, SHAMPOO_BETA * old + (1.0 - SHAMPOO_BETA) * term_v[ct, at], old
            )
    outs = [
        pltpu.make_async_copy(src, dst.at[0], out_sem.at[n])
        for n, (src, dst) in enumerate(
            ((left_v, left_out), (right_v, right_out), (moment_v, moment_out), (update_v, update_out))
        )
    ]
    for copy in outs:
        copy.start()
    pltpu.make_async_copy(norm_in, norm_in, norm_recv_sem).wait()
    for n in range(n_dp - 1):
        norms += norm_in[n]
    sums = jnp.broadcast_to(jnp.sum(norms, axis=1, keepdims=True), (8, LANES))
    slot = lax.broadcasted_iota(jnp.int32, (SIDE, LANES), 0)
    live = slot < jnp.full((SIDE, LANES), held, jnp.int32)
    scale = jnp.where(live, jnp.sqrt(sums[SIDE:] / jnp.where(live, sums[:SIDE], 1.0)), 0.0)
    scale_v[...] = scale
    last = pltpu.make_async_copy(scale_v, scale_out, out_sem.at[4])
    last.start()
    for copy in first + second:
        copy.wait_send()
    sent = gathered.at[pl.ds(0, SIDE - 1)]
    pltpu.make_async_copy(sent, sent, a_send_sem).wait()
    pltpu.make_async_copy(third, third, b_send_sem).wait()
    pltpu.make_async_copy(
        message.at[pl.ds(0, n_fsdp - 1)], message.at[pl.ds(0, n_fsdp - 1)], swap_send_sem
    ).wait()
    pltpu.make_async_copy(norm_in, norm_in, norm_send_sem).wait()
    for copy in outs + [last]:
        copy.wait()


def finish(left, right, moment, precond, scale, left_out, right_out, moment_out, update_out, held, sem):
    load = pltpu.make_async_copy(precond.at[0], held, sem.at[4])
    load.start()
    moves = [
        pltpu.make_async_copy(src, dst, sem.at[n])
        for n, (src, dst) in enumerate(((left, left_out), (right, right_out), (moment, moment_out)))
    ]
    for move in moves:
        move.start()
    load.wait()
    rows, order = held.shape[1:]
    for s in range(SIDE):
        held[s] = held[s] * jnp.broadcast_to(scale[s : s + 1, 0:1], (rows, order))
    last = pltpu.make_async_copy(held, update_out.at[0], sem.at[3])
    last.start()
    for move in moves + [last]:
        move.wait()


def on_device(
    grads, left_stats, right_stats, left_root, right_root, second_moment, slot_block, counts
):
    n_fsdp = lax.axis_size("fsdp")
    n_z = n_fsdp // 2
    blocks, slab = grads.shape[1:3]
    slots, rows, order = left_stats.shape[1:]
    quads = blocks // SIDE
    stack = slots * rows
    hbm = pl.BlockSpec(memory_space=pl.ANY)
    smem = pl.BlockSpec(memory_space=pltpu.SMEM)
    out = jax.ShapeDtypeStruct(left_stats.shape, F32)
    dma = pltpu.SemaphoreType.DMA
    vmem = pltpu.VMEM
    n_dp = SIDE * SIDE
    small = [pltpu.with_memory_space_constraint(a, pltpu.HBM) for a in (slot_block.T, counts)]
    pinned = [pltpu.with_memory_space_constraint(a, pltpu.HBM) for a in (grads, left_stats, right_stats, left_root, right_root, second_moment)]
    results = pl.pallas_call(
            functools.partial(kernel, n_fsdp, SPAN),
            out_shape=(out,) * 4 + (jax.ShapeDtypeStruct((SIDE, LANES), F32),),
            in_specs=[smem, smem] + [pl.BlockSpec(memory_space=pltpu.HBM)] * 6,
            out_specs=(hbm,) * 5,
            scratch_shapes=[
                vmem((blocks, slab, LANES), BF16),
                vmem((SIDE - 1, blocks, slab, LANES), BF16),
                vmem((quads * slab, SIDE * LANES), BF16),
                vmem((SIDE * LANES, SIDE * LANES), BF16),
                vmem((LANES, SIDE * LANES), BF16),
                vmem((SIDE, quads * slab, LANES), BF16),
                vmem((SIDE - 1, quads * slab, LANES), BF16),
                vmem((blocks + 1, slab, LANES), F32),
                vmem((n_fsdp, slab, LANES), BF16),
                vmem((n_dp, n_z, 2, slab, LANES), BF16),
                vmem((slots, rows, order), F32),
                vmem((slots, rows, order), F32),
                vmem((slots, rows, order), BF16),
                vmem((slots, order, order), BF16),
                vmem((slots, rows, order), F32),
                vmem((slots, rows, order), F32),
                vmem((slots, rows, order), F32),
                vmem((slots, rows, order), F32),
                vmem((slots, rows, order), F32),
                vmem((stack, order), BF16),
                vmem((SIDE, stack, LANES), BF16),
                vmem((SIDE, stack, LANES), F32),
                vmem((SIDE, stack, LANES), F32),
                vmem((8, LANES), F32),
                vmem((n_dp - 1, 8, LANES), F32),
                vmem((SIDE, LANES), F32),
                dma((6,)),
                dma((5,)),
                dma((SIDE - 1,)),
                dma((SIDE - 1,)),
                dma((SIDE - 1,)),
                dma((SIDE - 1,)),
                dma,
                dma((n_z // SPAN,)),
                dma,
                dma((n_z // SPAN, 2, SIDE - 1)),
                dma,
                dma,
                dma,
                dma,
                pltpu.SemaphoreType.REGULAR((4,)),
            ],
            compiler_params=pltpu.CompilerParams(
                collective_id=0, has_side_effects=True, vmem_limit_bytes=24 << 20
            ),
            name="shampoo",
        )(*small, *pinned)
    return tuple(
        pl.pallas_call(
            finish,
            out_shape=(out,) * 4,
            in_specs=[hbm] * 4 + [pl.BlockSpec(memory_space=pltpu.VMEM)],
            out_specs=(hbm,) * 4,
            scratch_shapes=[vmem((slots, rows, order), F32), dma((2 * 4,))],
            compiler_params=pltpu.CompilerParams(vmem_limit_bytes=4 << 20),
            name="finish",
        )(*results)
    )


def solution(mesh):
    in_specs = (
        P("dp", None, "fsdp", None),
        P("fsdp", None, "dp", None),
        P("fsdp", None, "dp", None),
        P("fsdp", None, "dp", None),
        P("fsdp", None, None, None),
        P("fsdp", None, "dp", None),
        P(),
        P(),
    )
    out_specs = (
        P("fsdp", None, "dp", None),
        P("fsdp", None, "dp", None),
        P("fsdp", None, "dp", None),
        P("fsdp", None, "dp", None),
    )
    return jax.shard_map(
        on_device, mesh=mesh, in_specs=in_specs, out_specs=out_specs, check_vma=False
    )
```

```python
import functools

import jax
import jax.numpy as jnp
from jax import lax
from jax.experimental import pallas as pl
from jax.experimental.pallas import tpu as pltpu
from jax.sharding import PartitionSpec as P

SHAMPOO_BETA = 0.998
ADAM_BETA = 0.95
EPSILON = 1e-08

SIDE = 4
LANES = 128
CHUNKS = 2
SPAN = 4
PART = LANES // SIDE
F32 = jnp.float32
BF16 = jnp.bfloat16


def kernel(
    n_fsdp,
    span,
    slot_ref,
    count_ref,
    grads,
    left_old,
    right_old,
    left_root,
    right_root,
    moment_old,
    left_out,
    right_out,
    moment_out,
    update_out,
    scale_out,
    own_tile,
    first_in,
    stacked,
    perm,
    rep,
    second_send,
    second_in,
    table,
    message,
    gathered,
    lo_v,
    ro_v,
    lr_v,
    rr_v,
    mo_v,
    left_v,
    right_v,
    moment_v,
    update_v,
    lhs_v,
    half_v,
    term_v,
    own_v,
    norm_out,
    norm_in,
    scale_v,
    load_sem,
    out_sem,
    first_send_sem,
    first_recv_sem,
    second_send_sem,
    second_recv_sem,
    swap_send_sem,
    swap_recv_sem,
    a_send_sem,
    a_recv_sem,
    b_send_sem,
    b_recv_sem,
    norm_send_sem,
    norm_recv_sem,
    met,
):
    dp = lax.axis_index("dp")
    owner = lax.axis_index("fsdp")
    gx, gy = dp // SIDE, dp % SIDE
    z, core = owner // 2, owner % 2
    n_z = n_fsdp // 2
    other = 1 - core
    i1 = gx * other + gy * core
    i2 = gy * other + gx * core

    def first_peer(k):
        return (((gx + k * other) % SIDE) * SIDE + (gy + k * core) % SIDE, owner)

    def second_peer(k):
        return (((gx + k * core) % SIDE) * SIDE + (gy + k * other) % SIDE, owner)

    def x_peer(k):
        return (((gx + k) % SIDE) * SIDE + gy, owner)

    def y_peer(k):
        return (gx * SIDE + (gy + k) % SIDE, owner)

    def z_peer(k):
        return (dp, ((z + k + n_z) % n_z) * 2 + core)

    def remote(src, dst, send, recv, peer):
        return pltpu.make_async_remote_copy(
            src_ref=src,
            dst_ref=dst,
            send_sem=send,
            recv_sem=recv,
            device_id=peer,
            device_id_type=pl.DeviceIdType.MESH,
        )

    own_load = pltpu.make_async_copy(
        grads.at[0, :, :, :, pl.ds(pl.multiple_of(i1 * LANES, LANES), LANES)], own_tile, load_sem.at[0]
    )
    own_load.start()

    barrier = pltpu.get_barrier_semaphore()
    greeted = [x_peer(k) for k in range(1, SIDE)] + [y_peer(k) for k in range(1, SIDE)]
    for k in (0, 1, -1, 2, -2):
        for c in (core, other):
            if k or c is other:
                greeted.append((dp, ((z + k + n_z) % n_z) * 2 + c))
    for peer in greeted:
        pl.semaphore_signal(barrier, inc=1, device_id=peer, device_id_type=pl.DeviceIdType.MESH)
    loads = [
        pltpu.make_async_copy(src.at[0], dst, load_sem.at[1 + n])
        for n, (src, dst) in enumerate(
            ((left_old, lo_v), (right_old, ro_v), (left_root, lr_v), (right_root, rr_v), (moment_old, mo_v))
        )
    ]
    for load in loads:
        load.start()
    pl.semaphore_wait(barrier, len(greeted))

    quads, slab = own_tile.shape[1:3]
    count = quads // CHUNKS
    first = []
    for ch in range(CHUNKS):
        for k in (2, 1, 3):
            tile = pl.ds(pl.multiple_of(((i1 + k) % SIDE) * LANES, LANES), LANES)
            copy = remote(
                grads.at[0, :, pl.ds(ch * count, count), :, tile],
                first_in.at[k - 1, :, pl.ds(ch * count, count)],
                first_send_sem.at[ch, k - 1],
                first_recv_sem.at[ch, k - 1],
                first_peer(k),
            )
            copy.start()
            first.append(copy)

    row = lax.broadcasted_iota(jnp.int32, (SIDE * LANES, SIDE * LANES), 0)
    col = lax.broadcasted_iota(jnp.int32, (SIDE * LANES, SIDE * LANES), 1)
    want = ((col % LANES) // PART) * LANES + (col // LANES) * PART + col % PART
    perm[...] = jnp.where(row == want, 1.0, 0.0).astype(BF16)
    row = lax.broadcasted_iota(jnp.int32, (LANES, SIDE * LANES), 0)
    col = lax.broadcasted_iota(jnp.int32, (LANES, SIDE * LANES), 1)
    rep[...] = jnp.where(row == (col // LANES) * PART + col % PART, 1.0, 0.0).astype(BF16)
    table[pl.ds(SIDE * 32, 1)] = jnp.zeros((1, 8, LANES), F32)

    reach = []
    k = 2
    while k < n_z // 2:
        reach.append(k)
        k *= 2

    def tell(n):
        for k in (reach[n], -reach[n]):
            pl.semaphore_signal(
                met.at[n], inc=1, device_id=z_peer(k), device_id_type=pl.DeviceIdType.MESH
            )

    tell(0)
    for n in range(1, len(reach)):
        pl.semaphore_wait(met.at[n - 1], 2)
        tell(n)

    own_load.wait()
    second = []
    for ch in range(CHUNKS):
        for copy in first[ch * (SIDE - 1) : (ch + 1) * (SIDE - 1)]:
            copy.wait_recv()
        some = slice(ch * count, (ch + 1) * count)
        lines = slice(ch * count * slab, (ch + 1) * count * slab)
        for i in range(SIDE):
            total = own_tile[i, some].astype(F32)
            for k in range(SIDE - 1):
                total += first_in[k, i, some].astype(F32)
            stacked[lines, i * LANES : (i + 1) * LANES] = total.reshape(count * slab, LANES).astype(BF16)
        packed = jnp.dot(stacked[lines, :], perm[...], preferred_element_type=F32)
        for q in range(SIDE):
            second_send[q, lines] = packed[:, q * LANES : (q + 1) * LANES].astype(BF16)
        for k in (2, 1, 3):
            copy = remote(
                second_send.at[(i2 + k) % SIDE, pl.ds(ch * count * slab, count * slab)],
                second_in.at[k - 1, pl.ds(ch * count * slab, count * slab)],
                second_send_sem.at[ch, k - 1],
                second_recv_sem.at[ch, k - 1],
                second_peer(k),
            )
            copy.start()
            second.append(copy)
    for ch in range(CHUNKS):
        for copy in second[ch * (SIDE - 1) : (ch + 1) * (SIDE - 1)]:
            copy.wait_recv()
        lines = slice(ch * count * slab, (ch + 1) * count * slab)
        total = second_send[i2, lines].astype(F32)
        for k in range(SIDE - 1):
            total += second_in[k, lines].astype(F32)
        spread = jnp.dot(total.astype(BF16), rep[...], preferred_element_type=F32)
        for i in range(SIDE):
            table[i * quads + ch * count : i * quads + (ch + 1) * count] = spread[
                :, i * LANES : (i + 1) * LANES
            ].reshape(count, slab, LANES)

    lane = lax.broadcasted_iota(jnp.int32, (8, LANES), 1) // PART

    def pick(o, carry):
        held = count_ref[o]
        value = jnp.zeros((8, LANES), F32)
        for s in range(SIDE):
            at = jnp.where(s < held, slot_ref[s, o], SIDE * quads)
            value = jnp.where(lane == s, table[at], value)
        message[o] = value.astype(BF16)
        return carry

    lax.fori_loop(0, n_fsdp, pick, 0, unroll=4)

    pl.semaphore_wait(met.at[len(reach) - 1], 2)
    mine = i1 * SIDE + i2
    zone = z // span
    keep = pltpu.make_async_copy(message.at[owner], gathered.at[mine, z, core], swap_recv_sem.at[zone])
    keep.start()

    def send_to(to):
        remote(
            message.at[to], gathered.at[mine, z, core], swap_send_sem, swap_recv_sem.at[zone], (dp, to)
        ).start()

    send_to(z * 2 + other)

    def swap(n, carry):
        for step in (n + 1, n_z - 1 - n):
            for c in range(2):
                send_to(((z + step) % n_z) * 2 + c)
        return carry

    lax.fori_loop(0, n_z // 2 - 1, swap, 0, unroll=5)
    for c in range(2):
        send_to(((z + n_z // 2) % n_z) * 2 + c)

    axes = ((gx, gy, x_peer, y_peer), (gy, gx, y_peer, x_peer))
    zones = n_z // span

    def along(parity, n, k, m, j1_back):
        j1, j2, one, two = axes[parity]
        at = pl.ds(pl.multiple_of(((zone + near_first[n]) % zones) * span, span), span)
        part = gathered.at[((j1 + SIDE - j1_back) % SIDE) * SIDE + j2, at, parity]
        if m:
            return remote(part, part, b_send_sem, b_recv_sem, two(m))
        return remote(part, part, a_send_sem, a_recv_sem.at[n, parity, k - 1], one(k))

    near_first = sorted(range(zones), key=lambda n: min(n, zones - n))

    def first_gather(n):
        here = (zone + near_first[n]) % zones
        whole = message.at[pl.ds(0, 2 * span)]
        pltpu.make_async_copy(whole, whole, swap_recv_sem.at[here]).wait()
        for k in (2, 1, 3):
            for parity in range(2):
                along(parity, n, k, 0, 0).start()
        for m in (2, 1, 3):
            for parity in range(2):
                along(parity, n, 0, m, 0).start()

    def second_gather(n):
        for k in (1, 3, 2):
            for parity in range(2):
                along(parity, n, k, 0, k).wait_recv()
                for m in (2, 1, 3):
                    along(parity, n, k, m, k).start()

    for n in range(zones):
        first_gather(n)
        if n:
            second_gather(n - 1)
    second_gather(zones - 1)
    third = gathered.at[pl.ds(0, SIDE * (SIDE - 1))]
    pltpu.make_async_copy(third, third, b_recv_sem).wait()

    for load in loads:
        load.wait()
    order = n_z * 16
    rows = lo_v.shape[1]
    own_rows = pl.ds(2 * dp, 2)

    def piece(p):
        return gathered[p].reshape(order, LANES)

    stack = SIDE * rows
    blockdiag = (
        lax.broadcasted_iota(jnp.int32, (stack, LANES), 0) // rows
        == lax.broadcasted_iota(jnp.int32, (stack, LANES), 1) // PART
    )
    lane_part = lax.broadcasted_iota(jnp.int32, (rows, LANES), 1) // PART
    held = count_ref[owner]

    def settle(value, s):
        result = jnp.zeros((rows, LANES), F32)
        for q in range(SIDE):
            block = value[q]
            shift = ((q - s) * PART) % LANES
            if shift:
                block = pltpu.roll(block, shift, axis=1)
            result = jnp.where(lane_part == q, block, result)
        return result

    def own_part(ct):
        return [gathered[ct * SIDE + q, own_rows].reshape(rows, LANES) for q in range(SIDE)]

    def wide_part(ct):
        return jnp.concatenate([piece(ct * SIDE + q) for q in range(SIDE)], axis=1)

    def halves(ct, carry):
        both = jnp.dot(lr_v[...].reshape(stack, order), wide_part(ct), preferred_element_type=F32)
        mine_rows = own_part(ct)
        for s in range(SIDE):
            at = slice(s * rows, (s + 1) * rows)
            half_v[ct, at] = settle([both[at, q * LANES : (q + 1) * LANES] for q in range(SIDE)], s).astype(BF16)
            own_v[ct, at] = settle([m.astype(F32) for m in mine_rows], s)
        return carry

    lax.fori_loop(0, SIDE, halves, 0)

    def terms(ct, left_sum):
        wide = wide_part(ct)
        both = jnp.dot(lhs_v[...], wide, preferred_element_type=F32)
        masked = jnp.concatenate(
            [
                jnp.where(blockdiag, jnp.concatenate([m.astype(F32)] * SIDE, axis=0), 0.0).astype(BF16)
                for m in own_part(ct)
            ],
            axis=1,
        )
        left_sum += lax.dot_general(masked, wide, (((1,), (1,)), ((), ())), preferred_element_type=F32)
        for s in range(SIDE):
            at = slice(s * rows, (s + 1) * rows)
            term_v[ct, at] = settle([both[at, q * LANES : (q + 1) * LANES] for q in range(SIDE)], s)
        return left_sum

    squares = []
    adams = []
    for s in range(SIDE):
        at = slice(s * rows, (s + 1) * rows)
        live = jnp.full((rows, LANES), s, jnp.int32) < jnp.full((rows, LANES), held, jnp.int32)
        precond = jnp.zeros((rows, order), F32)
        for ct in range(SIDE):
            precond += jnp.dot(
                half_v[ct, at], rr_v[s, ct * LANES : (ct + 1) * LANES, :], preferred_element_type=F32
            )
        update_v[s] = precond
        square = precond * precond
        lanes_sum = jnp.zeros((rows, LANES), F32)
        adam_sum = jnp.zeros((rows, LANES), F32)
        for ct in range(SIDE):
            here = slice(ct * LANES, (ct + 1) * LANES)
            lanes_sum += square[:, here]
            value = own_v[ct, at]
            old = mo_v[s, :, here]
            new = jnp.where(live, ADAM_BETA * old + (1.0 - ADAM_BETA) * value * value, old)
            moment_v[s, :, here] = new
            adam = value / (jnp.sqrt(new) + EPSILON)
            adam_sum += adam * adam
        squares.append(jnp.sum(lanes_sum, axis=0, keepdims=True))
        adams.append(jnp.sum(adam_sum, axis=0, keepdims=True))
    norms = jnp.concatenate(squares + adams, axis=0)
    norm_out[...] = norms

    n_dp = SIDE * SIDE

    def share(n, carry):
        to = ((dp + n + 1) % n_dp, owner)
        remote(norm_out, norm_in.at[n], norm_send_sem, norm_recv_sem, to).start()
        return carry

    lax.fori_loop(0, n_dp - 1, share, 0)
    lhs_v[...] = piece(dp).T
    left_sum = lax.fori_loop(0, SIDE, terms, jnp.zeros((stack, order), F32))
    for s in range(SIDE):
        at = slice(s * rows, (s + 1) * rows)
        live = jnp.full((rows, LANES), s, jnp.int32) < jnp.full((rows, LANES), held, jnp.int32)
        for ct in range(SIDE):
            here = slice(ct * LANES, (ct + 1) * LANES)
            old = lo_v[s, :, here]
            left_v[s, :, here] = jnp.where(
                live, SHAMPOO_BETA * old + (1.0 - SHAMPOO_BETA) * left_sum[at, here], old
            )
            old = ro_v[s, :, here]
            right_v[s, :, here] = jnp.where(
                live, SHAMPOO_BETA * old + (1.0 - SHAMPOO_BETA) * term_v[ct, at], old
            )
    outs = [
        pltpu.make_async_copy(src, dst.at[0], out_sem.at[n])
        for n, (src, dst) in enumerate(
            ((left_v, left_out), (right_v, right_out), (moment_v, moment_out), (update_v, update_out))
        )
    ]
    for copy in outs:
        copy.start()
    pltpu.make_async_copy(norm_in, norm_in, norm_recv_sem).wait()
    for n in range(n_dp - 1):
        norms += norm_in[n]
    sums = jnp.broadcast_to(jnp.sum(norms, axis=1, keepdims=True), (8, LANES))
    slot = lax.broadcasted_iota(jnp.int32, (SIDE, LANES), 0)
    live = slot < jnp.full((SIDE, LANES), held, jnp.int32)
    scale = jnp.where(live, jnp.sqrt(sums[SIDE:] / jnp.where(live, sums[:SIDE], 1.0)), 0.0)
    scale_v[...] = scale
    last = pltpu.make_async_copy(scale_v, scale_out, out_sem.at[4])
    last.start()
    for copy in first + second:
        copy.wait_send()
    sent = gathered.at[pl.ds(0, SIDE - 1)]
    pltpu.make_async_copy(sent, sent, a_send_sem).wait()
    pltpu.make_async_copy(third, third, b_send_sem).wait()
    pltpu.make_async_copy(
        message.at[pl.ds(0, n_fsdp - 1)], message.at[pl.ds(0, n_fsdp - 1)], swap_send_sem
    ).wait()
    pltpu.make_async_copy(norm_in, norm_in, norm_send_sem).wait()
    for copy in outs + [last]:
        copy.wait()


def finish(left, right, moment, precond, scale, left_out, right_out, moment_out, update_out, held, sem):
    load = pltpu.make_async_copy(precond.at[0], held, sem.at[4])
    load.start()
    moves = [
        pltpu.make_async_copy(src, dst, sem.at[n])
        for n, (src, dst) in enumerate(((left, left_out), (right, right_out), (moment, moment_out)))
    ]
    for move in moves:
        move.start()
    load.wait()
    rows, order = held.shape[1:]
    for s in range(SIDE):
        held[s] = held[s] * jnp.broadcast_to(scale[s : s + 1, 0:1], (rows, order))
    last = pltpu.make_async_copy(held, update_out.at[0], sem.at[3])
    last.start()
    for move in moves + [last]:
        move.wait()


def on_device(
    grads, left_stats, right_stats, left_root, right_root, second_moment, slot_block, counts
):
    n_fsdp = lax.axis_size("fsdp")
    n_z = n_fsdp // 2
    blocks, slab = grads.shape[1:3]
    slots, rows, order = left_stats.shape[1:]
    quads = blocks // SIDE
    stack = slots * rows
    hbm = pl.BlockSpec(memory_space=pl.ANY)
    smem = pl.BlockSpec(memory_space=pltpu.SMEM)
    out = jax.ShapeDtypeStruct(left_stats.shape, F32)
    dma = pltpu.SemaphoreType.DMA
    vmem = pltpu.VMEM
    n_dp = SIDE * SIDE
    small = [pltpu.with_memory_space_constraint(a, pltpu.HBM) for a in (slot_block.T, counts)]
    pinned = [pltpu.with_memory_space_constraint(a, pltpu.HBM) for a in (grads.reshape(1, SIDE, quads, slab, order), left_stats, right_stats, left_root, right_root, second_moment)]
    results = pl.pallas_call(
            functools.partial(kernel, n_fsdp, SPAN),
            out_shape=(out,) * 4 + (jax.ShapeDtypeStruct((SIDE, LANES), F32),),
            in_specs=[smem, smem] + [pl.BlockSpec(memory_space=pltpu.HBM)] * 6,
            out_specs=(hbm,) * 5,
            scratch_shapes=[
                vmem((SIDE, quads, slab, LANES), BF16),
                vmem((SIDE - 1, SIDE, quads, slab, LANES), BF16),
                vmem((quads * slab, SIDE * LANES), BF16),
                vmem((SIDE * LANES, SIDE * LANES), BF16),
                vmem((LANES, SIDE * LANES), BF16),
                vmem((SIDE, quads * slab, LANES), BF16),
                vmem((SIDE - 1, quads * slab, LANES), BF16),
                vmem((blocks + 1, slab, LANES), F32),
                vmem((n_fsdp, slab, LANES), BF16),
                vmem((n_dp, n_z, 2, slab, LANES), BF16),
                vmem((slots, rows, order), F32),
                vmem((slots, rows, order), F32),
                vmem((slots, rows, order), BF16),
                vmem((slots, order, order), BF16),
                vmem((slots, rows, order), F32),
                vmem((slots, rows, order), F32),
                vmem((slots, rows, order), F32),
                vmem((slots, rows, order), F32),
                vmem((slots, rows, order), F32),
                vmem((stack, order), BF16),
                vmem((SIDE, stack, LANES), BF16),
                vmem((SIDE, stack, LANES), F32),
                vmem((SIDE, stack, LANES), F32),
                vmem((8, LANES), F32),
                vmem((n_dp - 1, 8, LANES), F32),
                vmem((SIDE, LANES), F32),
                dma((6,)),
                dma((5,)),
                dma((CHUNKS, SIDE - 1)),
                dma((CHUNKS, SIDE - 1)),
                dma((CHUNKS, SIDE - 1)),
                dma((CHUNKS, SIDE - 1)),
                dma,
                dma((n_z // SPAN,)),
                dma,
                dma((n_z // SPAN, 2, SIDE - 1)),
                dma,
                dma,
                dma,
                dma,
                pltpu.SemaphoreType.REGULAR((4,)),
            ],
            compiler_params=pltpu.CompilerParams(
                collective_id=0, has_side_effects=True, vmem_limit_bytes=24 << 20
            ),
            name="shampoo",
        )(*small, *pinned)
    return tuple(
        pl.pallas_call(
            finish,
            out_shape=(out,) * 4,
            in_specs=[hbm] * 4 + [pl.BlockSpec(memory_space=pltpu.VMEM)],
            out_specs=(hbm,) * 4,
            scratch_shapes=[vmem((slots, rows, order), F32), dma((2 * 4,))],
            compiler_params=pltpu.CompilerParams(vmem_limit_bytes=4 << 20),
            name="finish",
        )(*results)
    )


def solution(mesh):
    in_specs = (
        P("dp", None, "fsdp", None),
        P("fsdp", None, "dp", None),
        P("fsdp", None, "dp", None),
        P("fsdp", None, "dp", None),
        P("fsdp", None, None, None),
        P("fsdp", None, "dp", None),
        P(),
        P(),
    )
    out_specs = (
        P("fsdp", None, "dp", None),
        P("fsdp", None, "dp", None),
        P("fsdp", None, "dp", None),
        P("fsdp", None, "dp", None),
    )
    return jax.shard_map(
        on_device, mesh=mesh, in_specs=in_specs, out_specs=out_specs, check_vma=False
    )
```

```python
import functools

import jax
import jax.numpy as jnp
from jax import lax
from jax.experimental import pallas as pl
from jax.experimental.pallas import tpu as pltpu
from jax.sharding import PartitionSpec as P

SHAMPOO_BETA = 0.998
ADAM_BETA = 0.95
EPSILON = 1e-08

SIDE = 4
LANES = 128
CHUNKS = 4
SPAN = 4
PART = LANES // SIDE
F32 = jnp.float32
BF16 = jnp.bfloat16


def kernel(
    n_fsdp,
    span,
    slot_ref,
    count_ref,
    grads,
    left_old,
    right_old,
    left_root,
    right_root,
    moment_old,
    left_out,
    right_out,
    moment_out,
    update_out,
    scale_out,
    own_tile,
    first_in,
    stacked,
    perm,
    rep,
    second_send,
    second_in,
    table,
    message,
    gathered,
    lo_v,
    ro_v,
    lr_v,
    rr_v,
    mo_v,
    left_v,
    right_v,
    moment_v,
    update_v,
    lhs_v,
    half_v,
    term_v,
    own_v,
    norm_out,
    norm_in,
    scale_v,
    load_sem,
    out_sem,
    first_send_sem,
    first_recv_sem,
    second_send_sem,
    second_recv_sem,
    swap_send_sem,
    swap_recv_sem,
    a_send_sem,
    a_recv_sem,
    b_send_sem,
    b_recv_sem,
    norm_send_sem,
    norm_recv_sem,
    met,
):
    dp = lax.axis_index("dp")
    owner = lax.axis_index("fsdp")
    gx, gy = dp // SIDE, dp % SIDE
    z, core = owner // 2, owner % 2
    n_z = n_fsdp // 2
    other = 1 - core
    i1 = gx * other + gy * core
    i2 = gy * other + gx * core

    def first_peer(k):
        return (((gx + k * other) % SIDE) * SIDE + (gy + k * core) % SIDE, owner)

    def second_peer(k):
        return (((gx + k * core) % SIDE) * SIDE + (gy + k * other) % SIDE, owner)

    def x_peer(k):
        return (((gx + k) % SIDE) * SIDE + gy, owner)

    def y_peer(k):
        return (gx * SIDE + (gy + k) % SIDE, owner)

    def z_peer(k):
        return (dp, ((z + k + n_z) % n_z) * 2 + core)

    def remote(src, dst, send, recv, peer):
        return pltpu.make_async_remote_copy(
            src_ref=src,
            dst_ref=dst,
            send_sem=send,
            recv_sem=recv,
            device_id=peer,
            device_id_type=pl.DeviceIdType.MESH,
        )

    own_load = pltpu.make_async_copy(
        grads.at[0, :, :, :, pl.ds(pl.multiple_of(i1 * LANES, LANES), LANES)], own_tile, load_sem.at[0]
    )
    own_load.start()

    barrier = pltpu.get_barrier_semaphore()
    greeted = [x_peer(k) for k in range(1, SIDE)] + [y_peer(k) for k in range(1, SIDE)]
    for k in (0, 1, -1, 2, -2):
        for c in (core, other):
            if k or c is other:
                greeted.append((dp, ((z + k + n_z) % n_z) * 2 + c))
    for peer in greeted:
        pl.semaphore_signal(barrier, inc=1, device_id=peer, device_id_type=pl.DeviceIdType.MESH)
    loads = [
        pltpu.make_async_copy(src.at[0], dst, load_sem.at[1 + n])
        for n, (src, dst) in enumerate(
            ((left_old, lo_v), (right_old, ro_v), (left_root, lr_v), (right_root, rr_v), (moment_old, mo_v))
        )
    ]
    for load in loads:
        load.start()
    pl.semaphore_wait(barrier, len(greeted))

    quads, slab = own_tile.shape[1:3]
    count = quads // CHUNKS
    first = []
    for ch in range(CHUNKS):
        for k in (2, 1, 3):
            tile = pl.ds(pl.multiple_of(((i1 + k) % SIDE) * LANES, LANES), LANES)
            copy = remote(
                grads.at[0, :, pl.ds(ch * count, count), :, tile],
                first_in.at[k - 1, :, pl.ds(ch * count, count)],
                first_send_sem.at[ch, k - 1],
                first_recv_sem.at[ch, k - 1],
                first_peer(k),
            )
            copy.start()
            first.append(copy)

    row = lax.broadcasted_iota(jnp.int32, (SIDE * LANES, SIDE * LANES), 0)
    col = lax.broadcasted_iota(jnp.int32, (SIDE * LANES, SIDE * LANES), 1)
    want = ((col % LANES) // PART) * LANES + (col // LANES) * PART + col % PART
    perm[...] = jnp.where(row == want, 1.0, 0.0).astype(BF16)
    row = lax.broadcasted_iota(jnp.int32, (LANES, SIDE * LANES), 0)
    col = lax.broadcasted_iota(jnp.int32, (LANES, SIDE * LANES), 1)
    rep[...] = jnp.where(row == (col // LANES) * PART + col % PART, 1.0, 0.0).astype(BF16)
    table[pl.ds(SIDE * 32, 1)] = jnp.zeros((1, 8, LANES), F32)

    reach = []
    k = 2
    while k < n_z // 2:
        reach.append(k)
        k *= 2

    def tell(n):
        for k in (reach[n], -reach[n]):
            pl.semaphore_signal(
                met.at[n], inc=1, device_id=z_peer(k), device_id_type=pl.DeviceIdType.MESH
            )

    tell(0)
    for n in range(1, len(reach)):
        pl.semaphore_wait(met.at[n - 1], 2)
        tell(n)

    own_load.wait()
    second = []
    for ch in range(CHUNKS):
        for copy in first[ch * (SIDE - 1) : (ch + 1) * (SIDE - 1)]:
            copy.wait_recv()
        some = slice(ch * count, (ch + 1) * count)
        lines = slice(ch * count * slab, (ch + 1) * count * slab)
        for i in range(SIDE):
            total = own_tile[i, some].astype(F32)
            for k in range(SIDE - 1):
                total += first_in[k, i, some].astype(F32)
            stacked[lines, i * LANES : (i + 1) * LANES] = total.reshape(count * slab, LANES).astype(BF16)
        packed = jnp.dot(stacked[lines, :], perm[...], preferred_element_type=F32)
        for q in range(SIDE):
            second_send[q, lines] = packed[:, q * LANES : (q + 1) * LANES].astype(BF16)
        for k in (2, 1, 3):
            copy = remote(
                second_send.at[(i2 + k) % SIDE, pl.ds(ch * count * slab, count * slab)],
                second_in.at[k - 1, pl.ds(ch * count * slab, count * slab)],
                second_send_sem.at[ch, k - 1],
                second_recv_sem.at[ch, k - 1],
                second_peer(k),
            )
            copy.start()
            second.append(copy)
    for ch in range(CHUNKS):
        for copy in second[ch * (SIDE - 1) : (ch + 1) * (SIDE - 1)]:
            copy.wait_recv()
        lines = slice(ch * count * slab, (ch + 1) * count * slab)
        total = second_send[i2, lines].astype(F32)
        for k in range(SIDE - 1):
            total += second_in[k, lines].astype(F32)
        spread = jnp.dot(total.astype(BF16), rep[...], preferred_element_type=F32)
        for i in range(SIDE):
            table[i * quads + ch * count : i * quads + (ch + 1) * count] = spread[
                :, i * LANES : (i + 1) * LANES
            ].reshape(count, slab, LANES)

    lane = lax.broadcasted_iota(jnp.int32, (8, LANES), 1) // PART

    def pick(o, carry):
        held = count_ref[o]
        value = jnp.zeros((8, LANES), F32)
        for s in range(SIDE):
            at = jnp.where(s < held, slot_ref[s, o], SIDE * quads)
            value = jnp.where(lane == s, table[at], value)
        message[o] = value.astype(BF16)
        return carry

    lax.fori_loop(0, n_fsdp, pick, 0, unroll=4)

    mine = i1 * SIDE + i2
    zone = z // span
    keep = pltpu.make_async_copy(message.at[owner], gathered.at[mine, z, core], swap_recv_sem.at[zone])
    keep.start()

    def send_to(to):
        remote(
            message.at[to], gathered.at[mine, z, core], swap_send_sem, swap_recv_sem.at[zone], (dp, to)
        ).start()

    send_to(z * 2 + other)

    def swap(n, carry):
        for step in (n + 1, n_z - 1 - n):
            for c in range(2):
                send_to(((z + step) % n_z) * 2 + c)
        return carry

    lax.fori_loop(0, reach[-1], swap, 0, unroll=4)
    pl.semaphore_wait(met.at[len(reach) - 1], 2)
    lax.fori_loop(reach[-1], n_z // 2 - 1, swap, 0, unroll=7)
    for c in range(2):
        send_to(((z + n_z // 2) % n_z) * 2 + c)

    axes = ((gx, gy, x_peer, y_peer), (gy, gx, y_peer, x_peer))
    zones = n_z // span

    def along(parity, n, k, m, j1_back):
        j1, j2, one, two = axes[parity]
        at = pl.ds(pl.multiple_of(((zone + near_first[n]) % zones) * span, span), span)
        part = gathered.at[((j1 + SIDE - j1_back) % SIDE) * SIDE + j2, at, parity]
        if m:
            return remote(part, part, b_send_sem, b_recv_sem, two(m))
        return remote(part, part, a_send_sem, a_recv_sem.at[n, parity, k - 1], one(k))

    near_first = sorted(range(zones), key=lambda n: min(n, zones - n))

    def first_gather(n):
        here = (zone + near_first[n]) % zones
        whole = message.at[pl.ds(0, 2 * span)]
        pltpu.make_async_copy(whole, whole, swap_recv_sem.at[here]).wait()
        for k in (2, 1, 3):
            for parity in range(2):
                along(parity, n, k, 0, 0).start()
        for m in (2, 1, 3):
            for parity in range(2):
                along(parity, n, 0, m, 0).start()

    def second_gather(n):
        for k in (1, 3, 2):
            for parity in range(2):
                along(parity, n, k, 0, k).wait_recv()
                for m in (2, 1, 3):
                    along(parity, n, k, m, k).start()

    for n in range(zones):
        first_gather(n)
        if n:
            second_gather(n - 1)
    second_gather(zones - 1)
    third = gathered.at[pl.ds(0, SIDE * (SIDE - 1))]
    pltpu.make_async_copy(third, third, b_recv_sem).wait()

    for load in loads:
        load.wait()
    order = n_z * 16
    rows = lo_v.shape[1]
    own_rows = pl.ds(2 * dp, 2)

    def piece(p):
        return gathered[p].reshape(order, LANES)

    stack = SIDE * rows
    blockdiag = (
        lax.broadcasted_iota(jnp.int32, (stack, LANES), 0) // rows
        == lax.broadcasted_iota(jnp.int32, (stack, LANES), 1) // PART
    )
    lane_part = lax.broadcasted_iota(jnp.int32, (rows, LANES), 1) // PART
    held = count_ref[owner]

    def settle(value, s):
        result = jnp.zeros((rows, LANES), F32)
        for q in range(SIDE):
            block = value[q]
            shift = ((q - s) * PART) % LANES
            if shift:
                block = pltpu.roll(block, shift, axis=1)
            result = jnp.where(lane_part == q, block, result)
        return result

    def own_part(ct):
        return [gathered[ct * SIDE + q, own_rows].reshape(rows, LANES) for q in range(SIDE)]

    def wide_part(ct):
        return jnp.concatenate([piece(ct * SIDE + q) for q in range(SIDE)], axis=1)

    def halves(ct, carry):
        both = jnp.dot(lr_v[...].reshape(stack, order), wide_part(ct), preferred_element_type=F32)
        mine_rows = own_part(ct)
        for s in range(SIDE):
            at = slice(s * rows, (s + 1) * rows)
            half_v[ct, at] = settle([both[at, q * LANES : (q + 1) * LANES] for q in range(SIDE)], s).astype(BF16)
            own_v[ct, at] = settle([m.astype(F32) for m in mine_rows], s)
        return carry

    lax.fori_loop(0, SIDE, halves, 0)

    def terms(ct, left_sum):
        wide = wide_part(ct)
        both = jnp.dot(lhs_v[...], wide, preferred_element_type=F32)
        masked = jnp.concatenate(
            [
                jnp.where(blockdiag, jnp.concatenate([m.astype(F32)] * SIDE, axis=0), 0.0).astype(BF16)
                for m in own_part(ct)
            ],
            axis=1,
        )
        left_sum += lax.dot_general(masked, wide, (((1,), (1,)), ((), ())), preferred_element_type=F32)
        for s in range(SIDE):
            at = slice(s * rows, (s + 1) * rows)
            term_v[ct, at] = settle([both[at, q * LANES : (q + 1) * LANES] for q in range(SIDE)], s)
        return left_sum

    squares = []
    adams = []
    for s in range(SIDE):
        at = slice(s * rows, (s + 1) * rows)
        live = jnp.full((rows, LANES), s, jnp.int32) < jnp.full((rows, LANES), held, jnp.int32)
        precond = jnp.zeros((rows, order), F32)
        for ct in range(SIDE):
            precond += jnp.dot(
                half_v[ct, at], rr_v[s, ct * LANES : (ct + 1) * LANES, :], preferred_element_type=F32
            )
        update_v[s] = precond
        square = precond * precond
        lanes_sum = jnp.zeros((rows, LANES), F32)
        adam_sum = jnp.zeros((rows, LANES), F32)
        for ct in range(SIDE):
            here = slice(ct * LANES, (ct + 1) * LANES)
            lanes_sum += square[:, here]
            value = own_v[ct, at]
            old = mo_v[s, :, here]
            new = jnp.where(live, ADAM_BETA * old + (1.0 - ADAM_BETA) * value * value, old)
            moment_v[s, :, here] = new
            adam = value / (jnp.sqrt(new) + EPSILON)
            adam_sum += adam * adam
        squares.append(jnp.sum(lanes_sum, axis=0, keepdims=True))
        adams.append(jnp.sum(adam_sum, axis=0, keepdims=True))
    norms = jnp.concatenate(squares + adams, axis=0)
    norm_out[...] = norms

    n_dp = SIDE * SIDE

    steps = [(kx, ky) for kx in range(SIDE) for ky in range(SIDE) if kx or ky]
    steps.sort(key=lambda k: -sum(min(n, SIDE - n) for n in k))
    for n, (kx, ky) in enumerate(steps):
        to = (((gx + kx) % SIDE) * SIDE + (gy + ky) % SIDE, owner)
        remote(norm_out, norm_in.at[n], norm_send_sem, norm_recv_sem, to).start()
    lhs_v[...] = piece(dp).T
    left_sum = lax.fori_loop(0, SIDE, terms, jnp.zeros((stack, order), F32))
    for s in range(SIDE):
        at = slice(s * rows, (s + 1) * rows)
        live = jnp.full((rows, LANES), s, jnp.int32) < jnp.full((rows, LANES), held, jnp.int32)
        for ct in range(SIDE):
            here = slice(ct * LANES, (ct + 1) * LANES)
            old = lo_v[s, :, here]
            left_v[s, :, here] = jnp.where(
                live, SHAMPOO_BETA * old + (1.0 - SHAMPOO_BETA) * left_sum[at, here], old
            )
            old = ro_v[s, :, here]
            right_v[s, :, here] = jnp.where(
                live, SHAMPOO_BETA * old + (1.0 - SHAMPOO_BETA) * term_v[ct, at], old
            )
    outs = [
        pltpu.make_async_copy(src, dst.at[0], out_sem.at[n])
        for n, (src, dst) in enumerate(
            ((left_v, left_out), (right_v, right_out), (moment_v, moment_out), (update_v, update_out))
        )
    ]
    for copy in outs:
        copy.start()
    pltpu.make_async_copy(norm_in, norm_in, norm_recv_sem).wait()
    for n in range(n_dp - 1):
        norms += norm_in[n]
    sums = jnp.broadcast_to(jnp.sum(norms, axis=1, keepdims=True), (8, LANES))
    slot = lax.broadcasted_iota(jnp.int32, (SIDE, LANES), 0)
    live = slot < jnp.full((SIDE, LANES), held, jnp.int32)
    scale = jnp.where(live, jnp.sqrt(sums[SIDE:] / jnp.where(live, sums[:SIDE], 1.0)), 0.0)
    scale_v[...] = scale
    last = pltpu.make_async_copy(scale_v, scale_out, out_sem.at[4])
    last.start()
    for copy in first + second:
        copy.wait_send()
    sent = gathered.at[pl.ds(0, SIDE - 1)]
    pltpu.make_async_copy(sent, sent, a_send_sem).wait()
    pltpu.make_async_copy(third, third, b_send_sem).wait()
    pltpu.make_async_copy(
        message.at[pl.ds(0, n_fsdp - 1)], message.at[pl.ds(0, n_fsdp - 1)], swap_send_sem
    ).wait()
    pltpu.make_async_copy(norm_in, norm_in, norm_send_sem).wait()
    for copy in outs + [last]:
        copy.wait()


def finish(left, right, moment, precond, scale, left_out, right_out, moment_out, update_out, held, sem):
    load = pltpu.make_async_copy(precond.at[0], held, sem.at[4])
    load.start()
    moves = [
        pltpu.make_async_copy(src, dst, sem.at[n])
        for n, (src, dst) in enumerate(((left, left_out), (right, right_out), (moment, moment_out)))
    ]
    for move in moves:
        move.start()
    load.wait()
    rows, order = held.shape[1:]
    for s in range(SIDE):
        held[s] = held[s] * jnp.broadcast_to(scale[s : s + 1, 0:1], (rows, order))
    last = pltpu.make_async_copy(held, update_out.at[0], sem.at[3])
    last.start()
    for move in moves + [last]:
        move.wait()


def on_device(
    grads, left_stats, right_stats, left_root, right_root, second_moment, slot_block, counts
):
    n_fsdp = lax.axis_size("fsdp")
    n_z = n_fsdp // 2
    blocks, slab = grads.shape[1:3]
    slots, rows, order = left_stats.shape[1:]
    quads = blocks // SIDE
    stack = slots * rows
    hbm = pl.BlockSpec(memory_space=pl.ANY)
    smem = pl.BlockSpec(memory_space=pltpu.SMEM)
    out = jax.ShapeDtypeStruct(left_stats.shape, F32)
    dma = pltpu.SemaphoreType.DMA
    vmem = pltpu.VMEM
    n_dp = SIDE * SIDE
    small = [pltpu.with_memory_space_constraint(a, pltpu.HBM) for a in (slot_block.T, counts)]
    pinned = [pltpu.with_memory_space_constraint(a, pltpu.HBM) for a in (grads.reshape(1, SIDE, quads, slab, order), left_stats, right_stats, left_root, right_root, second_moment)]
    results = pl.pallas_call(
            functools.partial(kernel, n_fsdp, SPAN),
            out_shape=(out,) * 4 + (jax.ShapeDtypeStruct((SIDE, LANES), F32),),
            in_specs=[smem, smem] + [pl.BlockSpec(memory_space=pltpu.HBM)] * 6,
            out_specs=(hbm,) * 5,
            scratch_shapes=[
                vmem((SIDE, quads, slab, LANES), BF16),
                vmem((SIDE - 1, SIDE, quads, slab, LANES), BF16),
                vmem((quads * slab, SIDE * LANES), BF16),
                vmem((SIDE * LANES, SIDE * LANES), BF16),
                vmem((LANES, SIDE * LANES), BF16),
                vmem((SIDE, quads * slab, LANES), BF16),
                vmem((SIDE - 1, quads * slab, LANES), BF16),
                vmem((blocks + 1, slab, LANES), F32),
                vmem((n_fsdp, slab, LANES), BF16),
                vmem((n_dp, n_z, 2, slab, LANES), BF16),
                vmem((slots, rows, order), F32),
                vmem((slots, rows, order), F32),
                vmem((slots, rows, order), BF16),
                vmem((slots, order, order), BF16),
                vmem((slots, rows, order), F32),
                vmem((slots, rows, order), F32),
                vmem((slots, rows, order), F32),
                vmem((slots, rows, order), F32),
                vmem((slots, rows, order), F32),
                vmem((stack, order), BF16),
                vmem((SIDE, stack, LANES), BF16),
                vmem((SIDE, stack, LANES), F32),
                vmem((SIDE, stack, LANES), F32),
                vmem((8, LANES), F32),
                vmem((n_dp - 1, 8, LANES), F32),
                vmem((SIDE, LANES), F32),
                dma((6,)),
                dma((5,)),
                dma((CHUNKS, SIDE - 1)),
                dma((CHUNKS, SIDE - 1)),
                dma((CHUNKS, SIDE - 1)),
                dma((CHUNKS, SIDE - 1)),
                dma,
                dma((n_z // SPAN,)),
                dma,
                dma((n_z // SPAN, 2, SIDE - 1)),
                dma,
                dma,
                dma,
                dma,
                pltpu.SemaphoreType.REGULAR((4,)),
            ],
            compiler_params=pltpu.CompilerParams(
                collective_id=0, has_side_effects=True, vmem_limit_bytes=24 << 20
            ),
            name="shampoo",
        )(*small, *pinned)
    return tuple(
        pl.pallas_call(
            finish,
            out_shape=(out,) * 4,
            in_specs=[hbm] * 4 + [pl.BlockSpec(memory_space=pltpu.VMEM)],
            out_specs=(hbm,) * 4,
            scratch_shapes=[vmem((slots, rows, order), F32), dma((2 * 4,))],
            compiler_params=pltpu.CompilerParams(vmem_limit_bytes=4 << 20),
            name="finish",
        )(*results)
    )


def solution(mesh):
    in_specs = (
        P("dp", None, "fsdp", None),
        P("fsdp", None, "dp", None),
        P("fsdp", None, "dp", None),
        P("fsdp", None, "dp", None),
        P("fsdp", None, None, None),
        P("fsdp", None, "dp", None),
        P(),
        P(),
    )
    out_specs = (
        P("fsdp", None, "dp", None),
        P("fsdp", None, "dp", None),
        P("fsdp", None, "dp", None),
        P("fsdp", None, "dp", None),
    )
    return jax.shard_map(
        on_device, mesh=mesh, in_specs=in_specs, out_specs=out_specs, check_vma=False
    )
```
